256 devices in a mesh: gx: 16 (over x, y), gy: 2 (over core), gz: 8 (over z).
Axes of the slice: x: 4, y: 4, z: 8, core: 2. Of those that a mesh axis runs over, the one named last changes fastest.
Arguments:
- field: float32 [2, 1024, 128, 1024], P(None, 'gx', 'gy', 'gz'), as said below
- start_basis: float32 [1024, 256], replicated, may hold values from -6 to 6
Outputs:
- factor: float32 [1024, 256], P('gx')
- core: float32 [2, 256, 128, 1024], P(None, 'gx', 'gy', 'gz')
The draws below stay inside these ranges and needn't reach their ends.
Inputs may be any that keep to these rules, and one draw needn't show every extreme that they name: Real-valued field; no structure is promised.
All inputs are finite; a program needn't handle non-finite values.
Results may differ from the reference program's by a relative error of at most 0.0002.
Values sent between devices are 32-bit elements; how exact they have to be, the bound alone decides.
A program may use at most 64 MiB of HBM per device.

```python
import jax
import jax.numpy as jnp
from jax import lax

MODE = 1024
RANK = 256
COMP = 2
ITERS = 2
NY = 128
NZ = 1024


def draw_field(key, part):
    key_rows = jax.random.fold_in(key, 11)
    key_cols = jax.random.fold_in(key, 12)
    key_vals = jax.random.fold_in(key, 13)
    row_scale = jnp.exp(jax.random.uniform(key_rows, (1, MODE, 1, 1), jnp.float32, 0.0, 1.386))
    col_scale = jnp.exp(jax.random.uniform(key_cols, (1, 1, NY, NZ), jnp.float32, -0.693, 0.693))
    values = 0.5 * jax.random.normal(key_vals, (COMP, MODE, NY, NZ), jnp.float32)
    return values * row_scale * col_scale


def normal_values(own_key, shape, width, most, dtype=jnp.bfloat16):
    return jnp.clip(width * jax.random.normal(own_key, shape, jnp.float32), -most, most).astype(dtype)


def setup_inputs(seed: int = 0) -> dict:
    splits = jax.random.split(jax.random.key(seed), 3)
    field = draw_field(jax.random.fold_in(splits[2], 71), 0)
    start_basis = normal_values(splits[1], (MODE, RANK), 1.0, 6.0, jnp.float32)
    return dict(field=field, start_basis=start_basis)


def orthonormal(image):
    small = jnp.dot(image.T, image, precision=lax.Precision.HIGHEST)
    lower = jnp.linalg.cholesky(small)
    return jax.scipy.linalg.solve_triangular(lower, image.T, lower=True).T

def reference(field, start_basis):
    unfold = field.reshape(COMP, MODE, NY * NZ)
    gram = jnp.einsum('crm,csm->rs', unfold, unfold, precision=lax.Precision.HIGHEST)
    basis = start_basis
    for step in range(ITERS):
        image = jnp.dot(gram, basis, precision=lax.Precision.HIGHEST)
        basis = orthonormal(image)
    core = jnp.einsum('rk,crm->ckm', basis, unfold, precision=lax.Precision.HIGHEST)
    return (basis, core.reshape(COMP, RANK, NY, NZ))
```

```python
import functools

import jax
import jax.numpy as jnp
from jax import lax
from jax.experimental import pallas as pl
from jax.experimental.pallas import tpu as pltpu
from jax.sharding import PartitionSpec as P

ITERS = 2
MODE = 1024
RANK = 256
PLANE = 16
DEPTH = 8
SLAB = MODE // PLANE
BLK = 256
SLOTS = [(a, b) for a in range(4) for b in range(a, 4)]
PACK = len(SLOTS) * 2 * BLK
HALF = PACK // 2
PIECE = HALF // PLANE
SUB = 24
MESH = pl.DeviceIdType.MESH
F32 = jnp.float32
BF16 = jnp.bfloat16
HI = lax.Precision.HIGHEST


def split(x):
    hi = x.astype(BF16)
    return hi, (x - hi.astype(F32)).astype(BF16)


def dot_nt(a, b):
    return lax.dot_general(a, b, (((1,), (1,)), ((), ())), preferred_element_type=F32)


def dot_nn(a, b, precision=None):
    return lax.dot_general(a, b, (((1,), (0,)), ((), ())), precision=precision, preferred_element_type=F32)


def dot_tn(a, b, precision=None):
    return lax.dot_general(a, b, (((0,), (0,)), ((), ())), precision=precision, preferred_element_type=F32)


def plane_peer(o):
    me = lax.axis_index("gx")
    x, y = me // 4, me % 4
    dx, dy = o // 4, o % 4
    to = ((x + dx) % 4) * 4 + (y + dy) % 4
    frm = ((x + 4 - dx) % 4) * 4 + (y + 4 - dy) % 4
    return to, frm


ORDER = (1, 3, 4, 12, 5, 7, 13, 15, 2, 8, 6, 14, 9, 11, 10)


def gram_kernel(field, h_out, l_out, g_out, fib, hs, ls, p, a1, r0, r1, a2, r2, a3, a4,
                s_fib, v_fib, s_0, v_0, s_1, v_1, s_2, v_2, s_3, v_3, s_4, v_4, s_5, v_5, loc):
    me = lax.axis_index("gx")
    core = lax.axis_index("gy")
    z = lax.axis_index("gz")
    barrier = pltpu.get_barrier_semaphore()
    for o in range(1, PLANE):
        pl.semaphore_signal(barrier, inc=1, device_id={"gx": plane_peer(o)[0]}, device_id_type=MESH)
    for o in range(1, DEPTH):
        pl.semaphore_signal(barrier, inc=1, device_id={"gz": (z + o) % DEPTH}, device_id_type=MESH)
    pl.semaphore_signal(barrier, inc=1, device_id={"gy": 1 - core}, device_id_type=MESH)
    pl.semaphore_wait(barrier, PLANE - 1 + DEPTH - 1 + 1)

    sends = []
    fib_copies = {}
    for o in ORDER:
        to, _ = plane_peer(o)
        c = pltpu.make_async_remote_copy(
            src_ref=field.at[to // 8, :, to % 8],
            dst_ref=fib.at[pl.ds(me * SLAB, SLAB)],
            send_sem=s_fib.at[o], recv_sem=v_fib.at[o],
            device_id={"gx": to}, device_id_type=MESH)
        c.start()
        fib_copies[o] = c
        sends.append(c)
    own = pltpu.make_async_copy(field.at[me // 8, :, me % 8], fib.at[pl.ds(me * SLAB, SLAB)], loc.at[0])
    own.start()
    a2[...] = jnp.zeros_like(a2)

    flat = fib.reshape(MODE * 8, 128)

    def halves(slab):
        for y in range(8):
            x = flat[pl.ds(slab * SLAB * 8 + y, SLAB, stride=8), :]
            hi, lo = split(x)
            hs[pl.ds(pl.multiple_of(slab * SLAB, SLAB), SLAB), y * 128:(y + 1) * 128] = hi
            ls[pl.ds(pl.multiple_of(slab * SLAB, SLAB), SLAB), y * 128:(y + 1) * 128] = lo

    own.wait()
    halves(me)
    for o in ORDER:
        fib_copies[o].wait_recv()
        halves(plane_peer(o)[1])

    keep_h = pltpu.make_async_copy(hs, h_out, loc.at[1])
    keep_l = pltpu.make_async_copy(ls, l_out, loc.at[2])
    keep_h.start()
    keep_l.start()

    for s, (a, b) in enumerate(SLOTS):
        ha, la = hs[a * BLK:(a + 1) * BLK, :], ls[a * BLK:(a + 1) * BLK, :]
        hb, lb = hs[b * BLK:(b + 1) * BLK, :], ls[b * BLK:(b + 1) * BLK, :]
        acc = dot_nt(ha, hb) + (dot_nt(ha, lb) + dot_nt(la, hb))
        p[s * 512:s * 512 + 256, :] = acc[:, :128]
        p[s * 512 + 256:s * 512 + 512, :] = acc[:, 128:]

    c = pltpu.make_async_remote_copy(
        src_ref=p.at[pl.ds((1 - core) * HALF, HALF)], dst_ref=r0, send_sem=s_0, recv_sem=v_0,
        device_id={"gy": 1 - core}, device_id_type=MESH)
    c.start()
    sends.append(c)
    c.wait_recv()
    mine = pl.multiple_of(core * HALF, HALF)
    a1[...] = p[pl.ds(mine, HALF), :] + r0[...]

    got = []
    for o in ORDER:
        to, _ = plane_peer(o)
        c = pltpu.make_async_remote_copy(
            src_ref=a1.at[pl.ds(to * PIECE, PIECE)], dst_ref=r1.at[o], send_sem=s_1.at[o], recv_sem=v_1.at[o],
            device_id={"gx": to}, device_id_type=MESH)
        c.start()
        got.append(c)
    acc = a1[pl.ds(pl.multiple_of(me * PIECE, PIECE), PIECE), :]
    for o, c in zip(ORDER, got):
        c.wait_recv()
        acc = acc + r1[o]
    sends += got
    a2[0:PIECE, :] = acc

    got = []
    for o in range(1, DEPTH):
        to = (z + o) % DEPTH
        c = pltpu.make_async_remote_copy(
            src_ref=a2.at[pl.ds(to * SUB, SUB)], dst_ref=r2.at[o], send_sem=s_2.at[o], recv_sem=v_2.at[o],
            device_id={"gz": to}, device_id_type=MESH)
        c.start()
        got.append(c)
    part = pl.ds(pl.multiple_of(z * SUB, SUB), SUB)
    acc = a2[part, :]
    for o, c in zip(range(1, DEPTH), got):
        c.wait_recv()
        acc = acc + r2[o]
    sends += got
    a3[...] = acc
    got = []
    for o in range(1, DEPTH):
        to = (z + o) % DEPTH
        c = pltpu.make_async_remote_copy(
            src_ref=a3, dst_ref=a4.at[part], send_sem=s_3.at[o], recv_sem=v_3.at[o],
            device_id={"gz": to}, device_id_type=MESH)
        c.start()
        got.append(c)
    a4[part, :] = acc
    for c in got:
        c.wait_recv()
    sends += got

    got = []
    piece = pl.ds(pl.multiple_of(mine + me * PIECE, PIECE), PIECE)
    for o in ORDER:
        to, _ = plane_peer(o)
        c = pltpu.make_async_remote_copy(
            src_ref=a4.at[pl.ds(0, PIECE)], dst_ref=g_out.at[piece], send_sem=s_4.at[o], recv_sem=v_4.at[o],
            device_id={"gx": to}, device_id_type=MESH)
        c.start()
        got.append(c)
    g_out[piece, :] = a4[0:PIECE, :]

    def forward(o, frm):
        rows = pl.ds(pl.multiple_of(mine + frm * PIECE, PIECE), PIECE)
        c = pltpu.make_async_remote_copy(
            src_ref=g_out.at[rows], dst_ref=g_out.at[rows], send_sem=s_5.at[o], recv_sem=v_5.at[o],
            device_id={"gy": 1 - core}, device_id_type=MESH)
        c.start()
        return c

    fwd = [forward(0, me)]
    for o, c in zip(ORDER, got):
        c.wait_recv()
        fwd.append(forward(o, plane_peer(o)[1]))
    for c in fwd:
        c.wait_recv()
    sends += got + fwd
    for c in sends:
        c.wait_send()
    keep_h.wait()
    keep_l.wait()


def gram_call(field):
    dma = pltpu.SemaphoreType.DMA
    vm = pltpu.VMEM
    return pl.pallas_call(
        gram_kernel,
        out_shape=(
            jax.ShapeDtypeStruct((MODE, 1024), BF16),
            jax.ShapeDtypeStruct((MODE, 1024), BF16),
            jax.ShapeDtypeStruct((PACK, 128), F32),
        ),
        in_specs=[pl.BlockSpec(memory_space=pl.ANY)],
        out_specs=(pl.BlockSpec(memory_space=pl.ANY), pl.BlockSpec(memory_space=pl.ANY),
                   pl.BlockSpec(memory_space=pltpu.VMEM)),
        scratch_shapes=[
            vm((MODE, 8, 128), F32), vm((MODE, 1024), BF16), vm((MODE, 1024), BF16),
            vm((PACK, 128), F32), vm((HALF, 128), F32), vm((HALF, 128), F32),
            vm((PLANE, PIECE, 128), F32), vm((DEPTH * SUB, 128), F32), vm((DEPTH, SUB, 128), F32),
            vm((SUB, 128), F32), vm((DEPTH * SUB, 128), F32),
            dma((PLANE,)), dma((PLANE,)), dma, dma, dma((PLANE,)), dma((PLANE,)),
            dma((DEPTH,)), dma((DEPTH,)), dma((DEPTH,)), dma((DEPTH,)),
            dma((PLANE,)), dma((PLANE,)), dma((PLANE,)), dma((PLANE,)), dma((3,)),
        ],
        compiler_params=pltpu.CompilerParams(
            collective_id=0, has_side_effects=True, vmem_limit_bytes=40 << 20),
        name="gram",
    )(field)


NB = 64


def lower_inverse(w):
    lane = lax.broadcasted_iota(jnp.int32, (8, 128), 1)
    row = lax.broadcasted_iota(jnp.int32, (8, 128), 0)
    nv = NB // 8
    for blk in range(RANK // NB):
        top = blk * NB
        chunk = (top // 128) * 128
        off = top - chunk
        d = [w[top + 8 * u:top + 8 * u + 8, chunk:chunk + 128] for u in range(nv)]
        scale = []
        for v in range(nv):
            e = {}
            for k in range(8):
                j = off + 8 * v + k
                for u in range(v, nv):
                    e[k, u] = jnp.broadcast_to(d[u][:, j:j + 1], (8, 128))
            dv = jnp.ones((8, 128), F32)
            for k in range(8):
                j = off + 8 * v + k
                piv = jnp.broadcast_to(e[k, v][k:k + 1, :], (8, 128))
                dv = jnp.where(row == k, piv, dv)
                inv = 1.0 / piv
                pivot_row = jnp.where(lane == j, 1.0, jnp.broadcast_to(d[v][k:k + 1, :], (8, 128)))
                for u in range(v, nv):
                    f = e[k, u] * inv
                    if u == v:
                        f = jnp.where(row > k, f, 0.0)
                        keep = jnp.where((lane == j) & (row > k), 0.0, d[u])
                    else:
                        keep = jnp.where(lane == j, 0.0, d[u])
                    d[u] = keep - f * pivot_row
                    for k2 in range(k + 1, 8):
                        b = jnp.broadcast_to(e[k2, v][k:k + 1, :], (8, 128))
                        e[k2, u] = e[k2, u] - f * b
            scale.append(lax.rsqrt(dv))
        part = []
        for u in range(nv):
            r = row + (off + 8 * u)
            inside = (lane >= off) & (lane < r)
            m = jnp.where(inside, d[u], jnp.where(lane == r, 1.0, 0.0)) * scale[u]
            part.append(m)
        linv = jnp.concatenate(part, axis=0)
        m = linv[:, off:off + NB]
        rows = w[top:top + NB, :]
        u_all = dot_nn(m, rows, HI)
        u_chunk = u_all[:, chunk:chunk + 128]
        lane_b = lax.broadcasted_iota(jnp.int32, (NB, 128), 1)
        mine = (lane_b >= off) & (lane_b < off + NB)
        u_chunk = jnp.where(mine, linv, u_chunk)
        if top + NB < RANK:
            left = dot_tn(u_all[:, top + NB:], u_all, HI)
            for c in range(0, RANK, 128):
                base = w[top + NB:, c:c + 128]
                if c == chunk:
                    lane_t = lax.broadcasted_iota(jnp.int32, base.shape, 1)
                    own = (lane_t >= off) & (lane_t < off + NB)
                    right = dot_tn(u_all[:, top + NB:], linv, HI)
                    w[top + NB:, c:c + 128] = jnp.where(own, -right, base - left[:, c:c + 128])
                else:
                    w[top + NB:, c:c + 128] = base - left[:, c:c + 128]
        for c in range(0, RANK, 128):
            w[top:top + NB, c:c + 128] = u_chunk if c == chunk else u_all[:, c:c + 128]


def basis_kernel(g_ref, b_ref, f_out, bh_out, bl_out, gh, gl, w):
    for s, (a, b) in enumerate(SLOTS):
        blk = jnp.concatenate([g_ref[s * 512:s * 512 + 256, :], g_ref[s * 512 + 256:s * 512 + 512, :]], axis=1)
        hi, lo = split(blk)
        gh[a * BLK:(a + 1) * BLK, b * BLK:(b + 1) * BLK] = hi
        gl[a * BLK:(a + 1) * BLK, b * BLK:(b + 1) * BLK] = lo
        if a != b:
            hi, lo = split(blk.T)
            gh[b * BLK:(b + 1) * BLK, a * BLK:(a + 1) * BLK] = hi
            gl[b * BLK:(b + 1) * BLK, a * BLK:(a + 1) * BLK] = lo
    basis = b_ref[...]
    lanes = lax.broadcasted_iota(jnp.int32, (RANK, RANK), 1)
    rows = lax.broadcasted_iota(jnp.int32, (RANK, RANK), 0)
    for step in range(ITERS):
        bh, bl = split(basis)
        image = dot_nn(gh[...], bh) + (dot_nn(gh[...], bl) + dot_nn(gl[...], bh))
        ih, il = split(image)
        w[...] = dot_tn(ih, ih) + (dot_tn(ih, il) + dot_tn(il, ih))
        lower_inverse(w)
        linv = jnp.where(lanes <= rows, w[...], 0.0)
        vh, vl = split(linv)
        if step < ITERS - 1:
            basis = dot_nt(ih, vh) + (dot_nt(ih, vl) + dot_nt(il, vh))
    basis = dot_nt(ih, vh) + (dot_nt(ih, vl) + dot_nt(il, vh))
    f_out[...] = basis
    bh, bl = split(basis.T)
    bh_out[...] = bh
    bl_out[...] = bl


def basis_call(packed, start):
    return pl.pallas_call(
        basis_kernel,
        out_shape=(
            jax.ShapeDtypeStruct((MODE, RANK), F32),
            jax.ShapeDtypeStruct((RANK, MODE), BF16),
            jax.ShapeDtypeStruct((RANK, MODE), BF16),
        ),
        scratch_shapes=[pltpu.VMEM((MODE, MODE), BF16), pltpu.VMEM((MODE, MODE), BF16),
                        pltpu.VMEM((RANK, RANK), F32)],
        compiler_params=pltpu.CompilerParams(vmem_limit_bytes=40 << 20),
        name="basis",
    )(packed, start)


def core_kernel(bh, bl, h, l, out, res, s_sem, v_sem, loc):
    me = lax.axis_index("gx")
    barrier = pltpu.get_barrier_semaphore()
    for o in range(1, PLANE):
        pl.semaphore_signal(barrier, inc=1, device_id={"gx": plane_peer(o)[0]}, device_id_type=MESH)
    flat = res.reshape(RANK * 8, 128)
    for yy in range(4):
        cols = slice(yy * 256, yy * 256 + 256)
        acc = dot_nn(bh[...], h[:, cols]) + (dot_nn(bh[...], l[:, cols]) + dot_nn(bl[...], h[:, cols]))
        flat[pl.ds(2 * yy, RANK, stride=8), :] = acc[:, :128]
        flat[pl.ds(2 * yy + 1, RANK, stride=8), :] = acc[:, 128:]
    pl.semaphore_wait(barrier, PLANE - 1)
    rank = RANK // PLANE
    copies = []
    for o in ORDER:
        to, _ = plane_peer(o)
        c = pltpu.make_async_remote_copy(
            src_ref=res.at[pl.ds(to * rank, rank)], dst_ref=out.at[me // 8, :, me % 8],
            send_sem=s_sem.at[o], recv_sem=v_sem.at[o], device_id={"gx": to}, device_id_type=MESH)
        c.start()
        copies.append(c)
    own = pltpu.make_async_copy(res.at[pl.ds(me * rank, rank)], out.at[me // 8, :, me % 8], loc)
    own.start()
    for c in copies:
        c.wait_recv()
    for c in copies:
        c.wait_send()
    own.wait()


def core_call(bh, bl, h, l, comps):
    vmem = pl.BlockSpec(memory_space=pltpu.VMEM)
    return pl.pallas_call(
        core_kernel,
        out_shape=jax.ShapeDtypeStruct((comps, RANK // PLANE, 8, 8, 128), F32),
        in_specs=[vmem] * 4,
        out_specs=pl.BlockSpec(memory_space=pl.ANY),
        scratch_shapes=[pltpu.VMEM((RANK, 8, 128), F32), pltpu.SemaphoreType.DMA((PLANE,)),
                        pltpu.SemaphoreType.DMA((PLANE,)), pltpu.SemaphoreType.DMA],
        compiler_params=pltpu.CompilerParams(
            collective_id=1, has_side_effects=True, vmem_limit_bytes=32 << 20),
        name="core",
    )(bh, bl, h, l)


def per_device(field, start_basis):
    comps, slab, cells_y, cells_z = field.shape
    h, l, packed = gram_call(field.reshape(comps, slab, cells_y // 8, 8, cells_z))
    basis, bh, bl = basis_call(packed, start_basis)
    core = core_call(bh, bl, h, l, comps)
    factor = lax.dynamic_slice_in_dim(basis, lax.axis_index("gx") * slab, slab, 0)
    return (factor, core.reshape(comps, RANK // PLANE, cells_y, cells_z))


def solution(mesh):
    placed = (P(None, "gx", "gy", "gz"), P())
    return jax.shard_map(
        per_device,
        mesh=mesh,
        in_specs=placed,
        out_specs=(P("gx", None), P(None, "gx", "gy", "gz")),
        check_vma=False,
    )
```

```python
import functools

import jax
import jax.numpy as jnp
from jax import lax
from jax.experimental import pallas as pl
from jax.experimental.pallas import tpu as pltpu
from jax.sharding import PartitionSpec as P

ITERS = 2
MODE = 1024
RANK = 256
PLANE = 16
DEPTH = 8
SLAB = MODE // PLANE
BLK = 256
SLOTS = [(a, b) for a in range(4) for b in range(a, 4)]
PACK = len(SLOTS) * 2 * BLK
HALF = PACK // 2
CHUNK = HALF // 2
PART = CHUNK // 2
QA = PART // 4
QB = QA // 4
SUB = 16
ROUNDS = 2
ZORDER = (4, 3, 5, 2, 6, 1, 7)
MESH = pl.DeviceIdType.MESH
F32 = jnp.float32
BF16 = jnp.bfloat16
HI = lax.Precision.HIGHEST


def split(x):
    hi = x.astype(BF16)
    return hi, (x - hi.astype(F32)).astype(BF16)


def dot_nt(a, b):
    return lax.dot_general(a, b, (((1,), (1,)), ((), ())), preferred_element_type=F32)


def dot_nn(a, b, precision=None):
    return lax.dot_general(a, b, (((1,), (0,)), ((), ())), precision=precision, preferred_element_type=F32)


def dot_tn(a, b, precision=None):
    return lax.dot_general(a, b, (((0,), (0,)), ((), ())), precision=precision, preferred_element_type=F32)


def plane_peer(o):
    me = lax.axis_index("gx")
    x, y = me // 4, me % 4
    dx, dy = o // 4, o % 4
    to = ((x + dx) % 4) * 4 + (y + dy) % 4
    frm = ((x + 4 - dx) % 4) * 4 + (y + 4 - dy) % 4
    return to, frm


ORDER = (1, 3, 4, 12, 5, 7, 13, 15, 2, 8, 6, 14, 9, 11, 10)
RING = (1, 3, 2)


def gram_kernel(field, hs, ls, g_out, fib, p, a1, r0, ra, a2, rb, zin, rz, a3, zout,
                s_fib, v_fib, s_0, v_0, s_a, v_a, s_b, v_b, s_z, v_z, s_w, v_w,
                s_c, v_c, s_d, v_d, s_5, v_5, loc):
    me = lax.axis_index("gx")
    core = lax.axis_index("gy")
    z = lax.axis_index("gz")
    x, y = me // 4, me % 4
    barrier = pltpu.get_barrier_semaphore()
    for o in range(1, PLANE):
        pl.semaphore_signal(barrier, inc=1, device_id={"gx": plane_peer(o)[0]}, device_id_type=MESH)
    for o in range(1, DEPTH):
        pl.semaphore_signal(barrier, inc=1, device_id={"gz": (z + o) % DEPTH}, device_id_type=MESH)
    pl.semaphore_signal(barrier, inc=1, device_id={"gy": 1 - core}, device_id_type=MESH)
    pl.semaphore_wait(barrier, PLANE - 1 + DEPTH - 1 + 1)

    sends = []

    def send(src, dst, s_sem, v_sem, device):
        c = pltpu.make_async_remote_copy(
            src_ref=src, dst_ref=dst, send_sem=s_sem, recv_sem=v_sem, device_id=device, device_id_type=MESH)
        c.start()
        sends.append(c)
        return c

    part = SLAB // ROUNDS
    arrivals = {}
    for r in range(ROUNDS):
        for o in ORDER:
            to, _ = plane_peer(o)
            arrivals[r, o] = send(
                field.at[to // 8, pl.ds(r * part, part), to % 8], fib.at[pl.ds(me * SLAB + r * part, part)],
                s_fib.at[r, o], v_fib.at[r, o], {"gx": to})
    own = pltpu.make_async_copy(field.at[me // 8, :, me % 8], fib.at[pl.ds(me * SLAB, SLAB)], loc)
    own.start()
    zin[...] = jnp.zeros_like(zin)

    flat = fib.reshape(MODE * 8, 128)

    def halves(slab, r):
        first = slab * SLAB + r * part
        rows = pl.ds(pl.multiple_of(first, part), part)
        for k in range(8):
            hi, lo = split(flat[pl.ds(first * 8 + k, part, stride=8), :])
            hs[rows, k * 128:(k + 1) * 128] = hi
            ls[rows, k * 128:(k + 1) * 128] = lo

    own.wait()
    for r in range(ROUNDS):
        halves(me, r)
    for r in range(ROUNDS):
        for o in ORDER:
            arrivals[r, o].wait_recv()
            halves(plane_peer(o)[1], r)

    def block(s):
        a, b = SLOTS[s]
        ha, la = hs[a * BLK:(a + 1) * BLK, :], ls[a * BLK:(a + 1) * BLK, :]
        hb, lb = hs[b * BLK:(b + 1) * BLK, :], ls[b * BLK:(b + 1) * BLK, :]
        acc = dot_nt(ha, hb) + (dot_nt(ha, lb) + dot_nt(la, hb))
        p[s * 512:s * 512 + 256, :] = acc[:, :128]
        p[s * 512 + 256:s * 512 + 512, :] = acc[:, 128:]

    mine = core * HALF
    other = {"gy": 1 - core}
    dims = ((x, y), (y, x))

    def ring(t, stage, o):
        if (t == 0) == (stage == 0):
            to = (x + o) % 4
            return {"gx": to * 4 + y}, to
        to = (y + o) % 4
        return {"gx": x * 4 + to}, to

    def reduce_chunk(c):
        base = c * CHUNK
        w = send(p.at[pl.ds((1 - core) * HALF + base, CHUNK)], r0.at[c], s_0.at[c], v_0.at[c], other)
        yield
        w.wait_recv()
        a1[c] = p[pl.ds(pl.multiple_of(mine + base, CHUNK), CHUNK), :] + r0[c]
        ws = []
        for o in RING:
            for t in range(2):
                dev, i = ring(t, 0, o)
                ws.append(send(a1.at[c, pl.ds(t * PART + i * QA, QA)], ra.at[c, t, o - 1],
                               s_a.at[c, t, o - 1], v_a.at[c, t, o - 1], dev))
        yield
        for w in ws:
            w.wait_recv()
        for t in range(2):
            a2[c, t] = (a1[c, pl.ds(pl.multiple_of(t * PART + dims[t][0] * QA, QA), QA), :]
                        + ra[c, t, 0] + ra[c, t, 1] + ra[c, t, 2])
        ws = []
        for o in RING:
            for t in range(2):
                dev, j = ring(t, 1, o)
                ws.append(send(a2.at[c, t, pl.ds(j * QB, QB)], rb.at[c, t, o - 1],
                               s_b.at[c, t, o - 1], v_b.at[c, t, o - 1], dev))
        yield
        for w in ws:
            w.wait_recv()
        for t in range(2):
            zin[c, t * QB:(t + 1) * QB, :] = (a2[c, t, pl.ds(pl.multiple_of(dims[t][1] * QB, QB), QB), :]
                                              + rb[c, t, 0] + rb[c, t, 1] + rb[c, t, 2])
        ws = []
        for o in ZORDER:
            to = (z + o) % DEPTH
            ws.append(send(zin.at[c, pl.ds(to * SUB, SUB)], rz.at[c, o], s_z.at[c, o], v_z.at[c, o], {"gz": to}))
        yield
        for w in ws:
            w.wait_recv()
        at = pl.ds(pl.multiple_of(z * SUB, SUB), SUB)
        acc = zin[c, at, :]
        for o in range(1, DEPTH):
            acc = acc + rz[c, o]
        a3[c] = acc
        ws = []
        for o in ZORDER:
            ws.append(send(a3.at[c], zout.at[c, at], s_w.at[c, o], v_w.at[c, o], {"gz": (z + o) % DEPTH}))
        zout[c, at, :] = acc
        yield
        for w in ws:
            w.wait_recv()
        ws = []
        for o in RING:
            for t in range(2):
                dev, _ = ring(t, 1, o)
                to = pl.ds(mine + base + t * PART + dims[t][0] * QA + dims[t][1] * QB, QB)
                ws.append(send(zout.at[c, pl.ds(t * QB, QB)], g_out.at[to],
                               s_c.at[c, t, o - 1], v_c.at[c, t, o - 1], dev))
        for t in range(2):
            to = pl.multiple_of(mine + base + t * PART + dims[t][0] * QA + dims[t][1] * QB, QB)
            g_out[pl.ds(to, QB), :] = zout[c, t * QB:(t + 1) * QB, :]
        yield
        for w in ws:
            w.wait_recv()
        ws = []
        for o in RING:
            for t in range(2):
                dev, _ = ring(t, 0, o)
                to = pl.ds(mine + base + t * PART + dims[t][0] * QA, QA)
                ws.append(send(g_out.at[to], g_out.at[to], s_d.at[c, t, o - 1], v_d.at[c, t, o - 1], dev))
        yield
        for w in ws:
            w.wait_recv()
        to = pl.ds(mine + base, CHUNK)
        w = send(g_out.at[to], g_out.at[to], s_5.at[c], v_5.at[c], other)
        yield
        w.wait_recv()
        yield

    one, two = reduce_chunk(0), reduce_chunk(1)
    for s in (0, 1, 2, 5, 6, 7):
        block(s)
    next(one)
    for s in (3, 4, 8, 9):
        block(s)
    next(two)
    for who in (one, two, one, one, two, one, two, one, two, one, two, two, one, two, one, two):
        next(who)
    for c in sends:
        c.wait_send()


def gram_call(field):
    dma = pltpu.SemaphoreType.DMA
    vm = pltpu.VMEM
    whole = pl.BlockSpec(memory_space=pltpu.VMEM)
    return pl.pallas_call(
        gram_kernel,
        out_shape=(
            jax.ShapeDtypeStruct((MODE, 1024), BF16),
            jax.ShapeDtypeStruct((MODE, 1024), BF16),
            jax.ShapeDtypeStruct((PACK, 128), F32),
        ),
        in_specs=[pl.BlockSpec(memory_space=pltpu.HBM)],
        out_specs=(whole, whole, whole),
        scratch_shapes=[
            vm((MODE, 8, 128), F32), vm((PACK, 128), F32), vm((2, CHUNK, 128), F32), vm((2, CHUNK, 128), F32),
            vm((2, 2, 3, QA, 128), F32), vm((2, 2, QA, 128), F32), vm((2, 2, 3, QB, 128), F32),
            vm((2, DEPTH * SUB, 128), F32), vm((2, DEPTH, SUB, 128), F32), vm((2, SUB, 128), F32),
            vm((2, DEPTH * SUB, 128), F32),
            dma((ROUNDS, PLANE)), dma((ROUNDS, PLANE)), dma((2,)), dma((2,)),
            dma((2, 2, 3)), dma((2, 2, 3)), dma((2, 2, 3)), dma((2, 2, 3)),
            dma((2, DEPTH)), dma((2, DEPTH)), dma((2, DEPTH)), dma((2, DEPTH)),
            dma((2, 2, 3)), dma((2, 2, 3)), dma((2, 2, 3)), dma((2, 2, 3)),
            dma((2,)), dma((2,)), dma,
        ],
        compiler_params=pltpu.CompilerParams(
            collective_id=0, has_side_effects=True, vmem_limit_bytes=40 << 20),
        name="gram",
    )(field)


NB = 64


def lower_inverse(w):
    lane = lax.broadcasted_iota(jnp.int32, (8, 128), 1)
    row = lax.broadcasted_iota(jnp.int32, (8, 128), 0)
    nv = NB // 8
    for blk in range(RANK // NB):
        top = blk * NB
        chunk = (top // 128) * 128
        off = top - chunk
        d = [w[top + 8 * u:top + 8 * u + 8, chunk:chunk + 128] for u in range(nv)]
        scale = []
        for v in range(nv):
            e = {}
            for k in range(8):
                j = off + 8 * v + k
                for u in range(v, nv):
                    e[k, u] = jnp.broadcast_to(d[u][:, j:j + 1], (8, 128))
            dv = jnp.ones((8, 128), F32)
            for k in range(8):
                j = off + 8 * v + k
                piv = jnp.broadcast_to(e[k, v][k:k + 1, :], (8, 128))
                dv = jnp.where(row == k, piv, dv)
                inv = 1.0 / piv
                pivot_row = jnp.where(lane == j, 1.0, jnp.broadcast_to(d[v][k:k + 1, :], (8, 128)))
                for u in range(v, nv):
                    f = e[k, u] * inv
                    if u == v:
                        f = jnp.where(row > k, f, 0.0)
                        keep = jnp.where((lane == j) & (row > k), 0.0, d[u])
                    else:
                        keep = jnp.where(lane == j, 0.0, d[u])
                    d[u] = keep - f * pivot_row
                    for k2 in range(k + 1, 8):
                        b = jnp.broadcast_to(e[k2, v][k:k + 1, :], (8, 128))
                        e[k2, u] = e[k2, u] - f * b
            scale.append(lax.rsqrt(dv))
        part = []
        for u in range(nv):
            r = row + (off + 8 * u)
            inside = (lane >= off) & (lane < r)
            m = jnp.where(inside, d[u], jnp.where(lane == r, 1.0, 0.0)) * scale[u]
            part.append(m)
        linv = jnp.concatenate(part, axis=0)
        m = linv[:, off:off + NB]
        rows = w[top:top + NB, :]
        u_all = dot_nn(m, rows, HI)
        u_chunk = u_all[:, chunk:chunk + 128]
        lane_b = lax.broadcasted_iota(jnp.int32, (NB, 128), 1)
        mine = (lane_b >= off) & (lane_b < off + NB)
        u_chunk = jnp.where(mine, linv, u_chunk)
        if top + NB < RANK:
            left = dot_tn(u_all[:, top + NB:], u_all, HI)
            for c in range(0, RANK, 128):
                base = w[top + NB:, c:c + 128]
                if c == chunk:
                    lane_t = lax.broadcasted_iota(jnp.int32, base.shape, 1)
                    own = (lane_t >= off) & (lane_t < off + NB)
                    right = dot_tn(u_all[:, top + NB:], linv, HI)
                    w[top + NB:, c:c + 128] = jnp.where(own, -right, base - left[:, c:c + 128])
                else:
                    w[top + NB:, c:c + 128] = base - left[:, c:c + 128]
        for c in range(0, RANK, 128):
            w[top:top + NB, c:c + 128] = u_chunk if c == chunk else u_all[:, c:c + 128]


def basis_kernel(g_ref, b_ref, f_out, bh_out, bl_out, gh, gl, w):
    for s, (a, b) in enumerate(SLOTS):
        blk = jnp.concatenate([g_ref[s * 512:s * 512 + 256, :], g_ref[s * 512 + 256:s * 512 + 512, :]], axis=1)
        hi, lo = split(blk)
        gh[a * BLK:(a + 1) * BLK, b * BLK:(b + 1) * BLK] = hi
        gl[a * BLK:(a + 1) * BLK, b * BLK:(b + 1) * BLK] = lo
        if a != b:
            hi, lo = split(blk.T)
            gh[b * BLK:(b + 1) * BLK, a * BLK:(a + 1) * BLK] = hi
            gl[b * BLK:(b + 1) * BLK, a * BLK:(a + 1) * BLK] = lo
    basis = b_ref[...]
    lanes = lax.broadcasted_iota(jnp.int32, (RANK, RANK), 1)
    rows = lax.broadcasted_iota(jnp.int32, (RANK, RANK), 0)
    for step in range(ITERS):
        bh, bl = split(basis)
        image = dot_nn(gh[...], bh) + (dot_nn(gh[...], bl) + dot_nn(gl[...], bh))
        ih, il = split(image)
        w[...] = dot_tn(ih, ih) + (dot_tn(ih, il) + dot_tn(il, ih))
        lower_inverse(w)
        linv = jnp.where(lanes <= rows, w[...], 0.0)
        vh, vl = split(linv)
        if step < ITERS - 1:
            basis = dot_nt(ih, vh) + (dot_nt(ih, vl) + dot_nt(il, vh))
    basis = dot_nt(ih, vh) + (dot_nt(ih, vl) + dot_nt(il, vh))
    f_out[...] = basis
    bh, bl = split(basis.T)
    bh_out[...] = bh
    bl_out[...] = bl


def basis_call(packed, start):
    return pl.pallas_call(
        basis_kernel,
        out_shape=(
            jax.ShapeDtypeStruct((MODE, RANK), F32),
            jax.ShapeDtypeStruct((RANK, MODE), BF16),
            jax.ShapeDtypeStruct((RANK, MODE), BF16),
        ),
        scratch_shapes=[pltpu.VMEM((MODE, MODE), BF16), pltpu.VMEM((MODE, MODE), BF16),
                        pltpu.VMEM((RANK, RANK), F32)],
        compiler_params=pltpu.CompilerParams(vmem_limit_bytes=40 << 20),
        name="basis",
    )(packed, start)


def core_kernel(bh, bl, h, l, out, res, s_sem, v_sem, loc):
    me = lax.axis_index("gx")
    barrier = pltpu.get_barrier_semaphore()
    for o in range(1, PLANE):
        pl.semaphore_signal(barrier, inc=1, device_id={"gx": plane_peer(o)[0]}, device_id_type=MESH)
    x = me // 4
    rank = RANK // PLANE
    wide = 4 * rank
    copies = []
    flat = res.reshape(RANK * 8, 128)
    for first, steps in enumerate(((1, 3), (2, 0))):
        places = [pl.multiple_of(((x + dx) % 4) * wide, wide) for dx in steps]
        rows_h = jnp.concatenate([bh[pl.ds(r, wide), :] for r in places], axis=0)
        rows_l = jnp.concatenate([bl[pl.ds(r, wide), :] for r in places], axis=0)
        for yy in range(4):
            cols = slice(yy * 256, yy * 256 + 256)
            acc = dot_nn(rows_h, h[:, cols]) + (dot_nn(rows_h, l[:, cols]) + dot_nn(rows_l, h[:, cols]))
            for n, r in enumerate(places):
                for e in range(2):
                    flat[pl.ds(r * 8 + 2 * yy + e, wide, stride=8), :] = (
                        acc[n * wide:(n + 1) * wide, e * 128:(e + 1) * 128])
        if first == 0:
            pl.semaphore_wait(barrier, PLANE - 1)
        for dy in (1, 3, 2, 0):
            for dx in steps:
                o = dx * 4 + dy
                if o == 0:
                    continue
                to, _ = plane_peer(o)
                c = pltpu.make_async_remote_copy(
                    src_ref=res.at[pl.ds(to * rank, rank)], dst_ref=out.at[me // 8, :, me % 8],
                    send_sem=s_sem.at[o], recv_sem=v_sem.at[o], device_id={"gx": to}, device_id_type=MESH)
                c.start()
                copies.append(c)
    own = pltpu.make_async_copy(res.at[pl.ds(me * rank, rank)], out.at[me // 8, :, me % 8], loc)
    own.start()
    for c in copies:
        c.wait_recv()
    for c in copies:
        c.wait_send()
    own.wait()


def core_call(bh, bl, h, l, comps):
    vmem = pl.BlockSpec(memory_space=pltpu.VMEM)
    return pl.pallas_call(
        core_kernel,
        out_shape=jax.ShapeDtypeStruct((comps, RANK // PLANE, 8, 8, 128), F32),
        in_specs=[vmem] * 4,
        out_specs=pl.BlockSpec(memory_space=pl.ANY),
        scratch_shapes=[pltpu.VMEM((RANK, 8, 128), F32), pltpu.SemaphoreType.DMA((PLANE,)),
                        pltpu.SemaphoreType.DMA((PLANE,)), pltpu.SemaphoreType.DMA],
        compiler_params=pltpu.CompilerParams(
            collective_id=1, has_side_effects=True, vmem_limit_bytes=32 << 20),
        name="core",
    )(bh, bl, h, l)


def per_device(field, start_basis):
    comps, slab, cells_y, cells_z = field.shape
    h, l, packed = gram_call(field.reshape(comps, slab, cells_y // 8, 8, cells_z))
    basis, bh, bl = basis_call(packed, start_basis)
    core = core_call(bh, bl, h, l, comps)
    factor = lax.dynamic_slice_in_dim(basis, lax.axis_index("gx") * slab, slab, 0)
    return (factor, core.reshape(comps, RANK // PLANE, cells_y, cells_z))


def solution(mesh):
    placed = (P(None, "gx", "gy", "gz"), P())
    return jax.shard_map(
        per_device,
        mesh=mesh,
        in_specs=placed,
        out_specs=(P("gx", None), P(None, "gx", "gy", "gz")),
        check_vma=False,
    )
```

```python
import functools

import jax
import jax.numpy as jnp
from jax import lax
from jax.experimental import pallas as pl
from jax.experimental.pallas import tpu as pltpu
from jax.sharding import PartitionSpec as P

ITERS = 2
MODE = 1024
RANK = 256
PLANE = 16
DEPTH = 8
SLAB = MODE // PLANE
BLK = 256
SLOTS = [(a, b) for a in range(4) for b in range(a, 4)]
PACK = len(SLOTS) * 2 * BLK
HALF = PACK // 2
CHUNK = HALF // 2
PART = CHUNK // 2
QA = PART // 4
QB = QA // 4
SUB = 16
ROUNDS = 2
ZORDER = (4, 3, 5, 2, 6, 1, 7)
MESH = pl.DeviceIdType.MESH
F32 = jnp.float32
BF16 = jnp.bfloat16
HI = lax.Precision.HIGHEST


def split(x):
    hi = x.astype(BF16)
    return hi, (x - hi.astype(F32)).astype(BF16)


def dot_nt(a, b):
    return lax.dot_general(a, b, (((1,), (1,)), ((), ())), preferred_element_type=F32)


def dot_nn(a, b, precision=None):
    return lax.dot_general(a, b, (((1,), (0,)), ((), ())), precision=precision, preferred_element_type=F32)


def dot_tn(a, b, precision=None):
    return lax.dot_general(a, b, (((0,), (0,)), ((), ())), precision=precision, preferred_element_type=F32)


def plane_peer(o):
    me = lax.axis_index("gx")
    x, y = me // 4, me % 4
    dx, dy = o // 4, o % 4
    to = ((x + dx) % 4) * 4 + (y + dy) % 4
    frm = ((x + 4 - dx) % 4) * 4 + (y + 4 - dy) % 4
    return to, frm


ORDER = (1, 3, 4, 12, 5, 7, 13, 15, 2, 8, 6, 14, 9, 11, 10)
RING = (1, 3, 2)


def gram_kernel(field, start, hs, ls, g_out, sh, sl, first, fib, p, a1, r0, ra, a2, rb, zin, rz, a3, zout,
                s_fib, v_fib, s_0, v_0, s_a, v_a, s_b, v_b, s_z, v_z, s_w, v_w,
                s_c, v_c, s_d, v_d, s_5, v_5, loc):
    me = lax.axis_index("gx")
    core = lax.axis_index("gy")
    z = lax.axis_index("gz")
    x, y = me // 4, me % 4
    barrier = pltpu.get_barrier_semaphore()
    for o in range(1, PLANE):
        pl.semaphore_signal(barrier, inc=1, device_id={"gx": plane_peer(o)[0]}, device_id_type=MESH)
    for o in range(1, DEPTH):
        pl.semaphore_signal(barrier, inc=1, device_id={"gz": (z + o) % DEPTH}, device_id_type=MESH)
    pl.semaphore_signal(barrier, inc=1, device_id={"gy": 1 - core}, device_id_type=MESH)
    pl.semaphore_wait(barrier, PLANE - 1 + DEPTH - 1 + 1)

    sends = []

    def send(src, dst, s_sem, v_sem, device):
        c = pltpu.make_async_remote_copy(
            src_ref=src, dst_ref=dst, send_sem=s_sem, recv_sem=v_sem, device_id=device, device_id_type=MESH)
        c.start()
        sends.append(c)
        return c

    part = SLAB // ROUNDS
    arrivals = {}
    for r in range(ROUNDS):
        for o in ORDER:
            to, _ = plane_peer(o)
            arrivals[r, o] = send(
                field.at[to // 8, pl.ds(r * part, part), to % 8], fib.at[pl.ds(me * SLAB + r * part, part)],
                s_fib.at[r, o], v_fib.at[r, o], {"gx": to})
    own = pltpu.make_async_copy(field.at[me // 8, :, me % 8], fib.at[pl.ds(me * SLAB, SLAB)], loc.at[0])
    own.start()
    begin = pltpu.make_async_copy(start, first, loc.at[1])
    begin.start()
    zin[...] = jnp.zeros_like(zin)

    flat = fib.reshape(MODE * 8, 128)

    def halves(slab, r):
        top = slab * SLAB + r * part
        rows = pl.ds(pl.multiple_of(top, part), part)
        for k in range(8):
            hi, lo = split(flat[pl.ds(top * 8 + k, part, stride=8), :])
            hs[rows, k * 128:(k + 1) * 128] = hi
            ls[rows, k * 128:(k + 1) * 128] = lo

    own.wait()
    for r in range(ROUNDS):
        halves(me, r)
    begin.wait()
    hi, lo = split(first[...].T)
    sh[...] = hi
    sl[...] = lo
    for r in range(ROUNDS):
        for o in ORDER:
            arrivals[r, o].wait_recv()
            halves(plane_peer(o)[1], r)

    def block(s):
        a, b = SLOTS[s]
        ha, la = hs[a * BLK:(a + 1) * BLK, :], ls[a * BLK:(a + 1) * BLK, :]
        hb, lb = hs[b * BLK:(b + 1) * BLK, :], ls[b * BLK:(b + 1) * BLK, :]
        acc = dot_nt(ha, hb) + (dot_nt(ha, lb) + dot_nt(la, hb))
        p[s * 512:s * 512 + 256, :] = acc[:, :128]
        p[s * 512 + 256:s * 512 + 512, :] = acc[:, 128:]

    mine = core * HALF
    other = {"gy": 1 - core}
    dims = ((x, y), (y, x))

    def ring(t, stage, o):
        if (t == 0) == (stage == 0):
            to = (x + o) % 4
            return {"gx": to * 4 + y}, to
        to = (y + o) % 4
        return {"gx": x * 4 + to}, to

    def reduce_chunk(c):
        base = c * CHUNK
        w = send(p.at[pl.ds((1 - core) * HALF + base, CHUNK)], r0.at[c], s_0.at[c], v_0.at[c], other)
        yield
        w.wait_recv()
        a1[c] = p[pl.ds(pl.multiple_of(mine + base, CHUNK), CHUNK), :] + r0[c]
        ws = []
        for o in RING:
            for t in range(2):
                dev, i = ring(t, 0, o)
                ws.append(send(a1.at[c, pl.ds(t * PART + i * QA, QA)], ra.at[c, t, o - 1],
                               s_a.at[c, t, o - 1], v_a.at[c, t, o - 1], dev))
        yield
        for w in ws:
            w.wait_recv()
        for t in range(2):
            a2[c, t] = (a1[c, pl.ds(pl.multiple_of(t * PART + dims[t][0] * QA, QA), QA), :]
                        + ra[c, t, 0] + ra[c, t, 1] + ra[c, t, 2])
        ws = []
        for o in RING:
            for t in range(2):
                dev, j = ring(t, 1, o)
                ws.append(send(a2.at[c, t, pl.ds(j * QB, QB)], rb.at[c, t, o - 1],
                               s_b.at[c, t, o - 1], v_b.at[c, t, o - 1], dev))
        yield
        for w in ws:
            w.wait_recv()
        for t in range(2):
            zin[c, t * QB:(t + 1) * QB, :] = (a2[c, t, pl.ds(pl.multiple_of(dims[t][1] * QB, QB), QB), :]
                                              + rb[c, t, 0] + rb[c, t, 1] + rb[c, t, 2])
        ws = []
        for o in ZORDER:
            to = (z + o) % DEPTH
            ws.append(send(zin.at[c, pl.ds(to * SUB, SUB)], rz.at[c, o], s_z.at[c, o], v_z.at[c, o], {"gz": to}))
        yield
        for w in ws:
            w.wait_recv()
        at = pl.ds(pl.multiple_of(z * SUB, SUB), SUB)
        acc = zin[c, at, :]
        for o in range(1, DEPTH):
            acc = acc + rz[c, o]
        a3[c] = acc
        ws = []
        for o in ZORDER:
            ws.append(send(a3.at[c], zout.at[c, at], s_w.at[c, o], v_w.at[c, o], {"gz": (z + o) % DEPTH}))
        zout[c, at, :] = acc
        yield
        for w in ws:
            w.wait_recv()
        ws = []
        for o in RING:
            for t in range(2):
                dev, _ = ring(t, 1, o)
                to = pl.ds(mine + base + t * PART + dims[t][0] * QA + dims[t][1] * QB, QB)
                ws.append(send(zout.at[c, pl.ds(t * QB, QB)], g_out.at[to],
                               s_c.at[c, t, o - 1], v_c.at[c, t, o - 1], dev))
        for t in range(2):
            to = pl.multiple_of(mine + base + t * PART + dims[t][0] * QA + dims[t][1] * QB, QB)
            g_out[pl.ds(to, QB), :] = zout[c, t * QB:(t + 1) * QB, :]
        yield
        for w in ws:
            w.wait_recv()
        ws = []
        for o in RING:
            for t in range(2):
                dev, _ = ring(t, 0, o)
                to = pl.ds(mine + base + t * PART + dims[t][0] * QA, QA)
                ws.append(send(g_out.at[to], g_out.at[to], s_d.at[c, t, o - 1], v_d.at[c, t, o - 1], dev))

        def forward(i, t, o):
            at = pl.ds(mine + base + t * PART + i * QA, QA)
            return send(g_out.at[at], g_out.at[at], s_5.at[c, t, o], v_5.at[c, t, o], other)

        early = [forward(dims[t][0], t, 0) for t in range(2)]
        yield
        last = []
        for w, (o, t) in zip(ws, [(o, t) for o in RING for t in range(2)]):
            w.wait_recv()
            last.append(forward((dims[t][0] + 4 - o) % 4, t, o))
        yield
        for w in early + last:
            w.wait_recv()
        yield

    one, two = reduce_chunk(0), reduce_chunk(1)
    for s in (0, 1, 2, 5, 6, 7):
        block(s)
    next(one)
    for s in (3, 4):
        block(s)
    next(one)
    for s in (8, 9):
        block(s)
    next(two)
    for who in (one, two, one, two, one, two, one, two, one, two, two, one, two, one, two):
        next(who)
    for c in sends:
        c.wait_send()


def gram_call(field, start):
    dma = pltpu.SemaphoreType.DMA
    vm = pltpu.VMEM
    whole = pl.BlockSpec(memory_space=pltpu.VMEM)
    return pl.pallas_call(
        gram_kernel,
        out_shape=(
            jax.ShapeDtypeStruct((MODE, 1024), BF16),
            jax.ShapeDtypeStruct((MODE, 1024), BF16),
            jax.ShapeDtypeStruct((PACK, 128), F32),
            jax.ShapeDtypeStruct((RANK, MODE), BF16),
            jax.ShapeDtypeStruct((RANK, MODE), BF16),
        ),
        in_specs=[pl.BlockSpec(memory_space=pltpu.HBM)] * 2,
        out_specs=(whole,) * 5,
        scratch_shapes=[
            vm((MODE, RANK), F32), vm((MODE, 8, 128), F32), vm((PACK, 128), F32), vm((2, CHUNK, 128), F32), vm((2, CHUNK, 128), F32),
            vm((2, 2, 3, QA, 128), F32), vm((2, 2, QA, 128), F32), vm((2, 2, 3, QB, 128), F32),
            vm((2, DEPTH * SUB, 128), F32), vm((2, DEPTH, SUB, 128), F32), vm((2, SUB, 128), F32),
            vm((2, DEPTH * SUB, 128), F32),
            dma((ROUNDS, PLANE)), dma((ROUNDS, PLANE)), dma((2,)), dma((2,)),
            dma((2, 2, 3)), dma((2, 2, 3)), dma((2, 2, 3)), dma((2, 2, 3)),
            dma((2, DEPTH)), dma((2, DEPTH)), dma((2, DEPTH)), dma((2, DEPTH)),
            dma((2, 2, 3)), dma((2, 2, 3)), dma((2, 2, 3)), dma((2, 2, 3)),
            dma((2, 2, 4)), dma((2, 2, 4)), dma((2,)),
        ],
        compiler_params=pltpu.CompilerParams(
            collective_id=0, has_side_effects=True, vmem_limit_bytes=40 << 20),
        name="gram",
    )(field, start)


NB = 64


def recip(x):
    return 1.0 / x


def row_of(x, k):
    return jnp.broadcast_to(x[k:k + 1, :], (8, 128))


def lower_inverse(w):
    lane = lax.broadcasted_iota(jnp.int32, (8, 128), 1)
    row = lax.broadcasted_iota(jnp.int32, (8, 128), 0)
    nv = NB // 8
    chunks = RANK // 128
    for top in range(0, RANK, NB):
        pc = top // 128
        off = top % 128
        d = [[w[top + 8 * u:top + 8 * u + 8, c * 128:(c + 1) * 128] for c in range(chunks)] for u in range(nv)]
        scale = []
        for v in range(nv):
            j0 = off + 8 * v
            e = [jnp.broadcast_to(d[v][pc][:, j0 + k:j0 + k + 1], (8, 128)) for k in range(8)]
            group = (lane >= j0) & (lane < j0 + 8)
            inv, b = [], {}
            dv = jnp.ones((8, 128), F32)
            for k in range(8):
                piv = row_of(e[k], k)
                dv = jnp.where(row == k, piv, dv)
                inv.append(recip(piv))
                f = jnp.where(row > k, e[k] * inv[k], 0.0)
                for k2 in range(k + 1, 8):
                    b[k, k2] = row_of(e[k2], k)
                    e[k2] = e[k2] - f * b[k, k2]
                for c in range(chunks):
                    prow = row_of(d[v][c], k)
                    if c == pc:
                        prow = jnp.where(lane == j0 + k, 1.0, prow)
                        base = jnp.where((lane == j0 + k) & (row > k), 0.0, d[v][c])
                    else:
                        base = d[v][c]
                    d[v][c] = base - f * prow
            scale.append(lax.rsqrt(dv))
            unit = jnp.where(lane == j0 + row, 1.0, jnp.where(lane < j0 + row, d[v][pc], 0.0))
            d[v][pc] = jnp.where(group, unit, d[v][pc])
            for u in range(v + 1, nv):
                e = [jnp.broadcast_to(d[u][pc][:, j0 + k:j0 + k + 1], (8, 128)) for k in range(8)]
                f = []
                for k in range(8):
                    f.append(e[k] * inv[k])
                    for k2 in range(k + 1, 8):
                        e[k2] = e[k2] - f[k] * b[k, k2]
                for c in range(chunks):
                    t = f[0] * row_of(d[v][c], 0)
                    for k in range(1, 8):
                        t = t + f[k] * row_of(d[v][c], k)
                    d[u][c] = (jnp.where(group, 0.0, d[u][c]) if c == pc else d[u][c]) - t
        cols = []
        for c in range(chunks):
            rows = []
            for u in range(nv):
                x = d[u][c]
                if c == pc:
                    x = jnp.where((lane > off + 8 * u + row) & (lane < off + NB), 0.0, x)
                rows.append(x * scale[u])
            cols.append(jnp.concatenate(rows, axis=0))
        done = jnp.concatenate(cols, axis=1)
        w[top:top + NB, :] = done
        if top + NB < RANK:
            hi, lo = split(done)
            left = jnp.concatenate([hi, hi, lo], axis=0)[:, top + NB:]
            t = dot_tn(left, jnp.concatenate([hi, lo, hi], axis=0))
            for c in range(chunks):
                base = w[top + NB:, c * 128:(c + 1) * 128]
                if c == pc:
                    at = lax.broadcasted_iota(jnp.int32, base.shape, 1)
                    base = jnp.where((at >= off) & (at < off + NB), 0.0, base)
                w[top + NB:, c * 128:(c + 1) * 128] = base - t[:, c * 128:(c + 1) * 128]


def basis_kernel(g_ref, sh_ref, sl_ref, f_out, bh_out, bl_out, gh, gl, w, wide):
    for s, (a, b) in enumerate(SLOTS):
        for e in range(2):
            hi, lo = split(g_ref[s * 512 + e * 256:s * 512 + e * 256 + 256, :])
            cols = slice(b * BLK + e * 128, b * BLK + e * 128 + 128)
            gh[a * BLK:(a + 1) * BLK, cols] = hi
            gl[a * BLK:(a + 1) * BLK, cols] = lo
    lanes = lax.broadcasted_iota(jnp.int32, (RANK, RANK), 1)
    rows = lax.broadcasted_iota(jnp.int32, (RANK, RANK), 0)
    bh, bl = sh_ref[...], sl_ref[...]
    for step in range(ITERS):
        image = []
        for b in range(4):
            n = (b + 1) * BLK
            cols = slice(b * BLK, n)
            acc = (dot_nn(bh[:, :n], gh[:n, cols])
                   + (dot_nn(bh[:, :n], gl[:n, cols]) + dot_nn(bl[:, :n], gh[:n, cols])))
            if n < MODE:
                acc = acc + (dot_nt(bh[:, n:], gh[cols, n:])
                             + (dot_nt(bh[:, n:], gl[cols, n:]) + dot_nt(bl[:, n:], gh[cols, n:])))
            image.append(acc)
        ih, il = split(jnp.concatenate(image, axis=1))
        w[...] = dot_nt(ih, ih) + (dot_nt(ih, il) + dot_nt(il, ih))
        lower_inverse(w)
        vh, vl = split(jnp.where(lanes <= rows, w[...], 0.0))
        basis = dot_nn(vh, ih) + (dot_nn(vh, il) + dot_nn(vl, ih))
        bh, bl = split(basis)
    bh_out[...] = bh
    bl_out[...] = bl
    me = lax.axis_index("gx")
    wide[...] = basis
    pair = wide[:, pl.ds(pl.multiple_of((me // 2) * 128, 128), 128)].T
    f_out[...] = jnp.where(me % 2 == 0, pair[:SLAB, :], pair[SLAB:, :])


def basis_call(packed, start_h, start_l):
    return pl.pallas_call(
        basis_kernel,
        out_shape=(
            jax.ShapeDtypeStruct((SLAB, RANK), F32),
            jax.ShapeDtypeStruct((RANK, MODE), BF16),
            jax.ShapeDtypeStruct((RANK, MODE), BF16),
        ),
        scratch_shapes=[pltpu.VMEM((MODE, MODE), BF16), pltpu.VMEM((MODE, MODE), BF16),
                        pltpu.VMEM((RANK, RANK), F32), pltpu.VMEM((RANK, MODE), F32)],
        compiler_params=pltpu.CompilerParams(vmem_limit_bytes=40 << 20),
        name="basis",
    )(packed, start_h, start_l)


def core_kernel(bh, bl, h, l, out, res, s_sem, v_sem, loc):
    me = lax.axis_index("gx")
    barrier = pltpu.get_barrier_semaphore()
    for o in range(1, PLANE):
        pl.semaphore_signal(barrier, inc=1, device_id={"gx": plane_peer(o)[0]}, device_id_type=MESH)
    x = me // 4
    rank = RANK // PLANE
    wide = 4 * rank
    copies = []
    flat = res.reshape(RANK * 8, 128)
    for first, steps in enumerate(((1, 3), (2, 0))):
        places = [pl.multiple_of(((x + dx) % 4) * wide, wide) for dx in steps]
        rows_h = jnp.concatenate([bh[pl.ds(r, wide), :] for r in places], axis=0)
        rows_l = jnp.concatenate([bl[pl.ds(r, wide), :] for r in places], axis=0)
        for yy in range(4):
            cols = slice(yy * 256, yy * 256 + 256)
            acc = dot_nn(rows_h, h[:, cols]) + (dot_nn(rows_h, l[:, cols]) + dot_nn(rows_l, h[:, cols]))
            for n, r in enumerate(places):
                for e in range(2):
                    flat[pl.ds(r * 8 + 2 * yy + e, wide, stride=8), :] = (
                        acc[n * wide:(n + 1) * wide, e * 128:(e + 1) * 128])
        if first == 0:
            pl.semaphore_wait(barrier, PLANE - 1)
        for dy in (1, 3, 2, 0):
            for dx in steps:
                o = dx * 4 + dy
                if o == 0:
                    continue
                to, _ = plane_peer(o)
                c = pltpu.make_async_remote_copy(
                    src_ref=res.at[pl.ds(to * rank, rank)], dst_ref=out.at[me // 8, :, me % 8],
                    send_sem=s_sem.at[o], recv_sem=v_sem.at[o], device_id={"gx": to}, device_id_type=MESH)
                c.start()
                copies.append(c)
    own = pltpu.make_async_copy(res.at[pl.ds(me * rank, rank)], out.at[me // 8, :, me % 8], loc)
    own.start()
    for c in copies:
        c.wait_recv()
    for c in copies:
        c.wait_send()
    own.wait()


def core_call(bh, bl, h, l, comps):
    vmem = pl.BlockSpec(memory_space=pltpu.VMEM)
    return pl.pallas_call(
        core_kernel,
        out_shape=jax.ShapeDtypeStruct((comps, RANK // PLANE, 8, 8, 128), F32),
        in_specs=[vmem] * 4,
        out_specs=pl.BlockSpec(memory_space=pl.ANY),
        scratch_shapes=[pltpu.VMEM((RANK, 8, 128), F32), pltpu.SemaphoreType.DMA((PLANE,)),
                        pltpu.SemaphoreType.DMA((PLANE,)), pltpu.SemaphoreType.DMA],
        compiler_params=pltpu.CompilerParams(
            collective_id=1, has_side_effects=True, vmem_limit_bytes=32 << 20),
        name="core",
    )(bh, bl, h, l)


def per_device(field, start_basis):
    comps, slab, cells_y, cells_z = field.shape
    h, l, packed, start_h, start_l = gram_call(
        pltpu.with_memory_space_constraint(field.reshape(comps, slab, cells_y // 8, 8, cells_z), pltpu.HBM),
        pltpu.with_memory_space_constraint(start_basis, pltpu.HBM))
    factor, bh, bl = basis_call(packed, start_h, start_l)
    core = core_call(bh, bl, h, l, comps)
    return (factor, core.reshape(comps, RANK // PLANE, cells_y, cells_z))


def solution(mesh):
    placed = (P(None, "gx", "gy", "gz"), P())
    return jax.shard_map(
        per_device,
        mesh=mesh,
        in_specs=placed,
        out_specs=(P("gx", None), P(None, "gx", "gy", "gz")),
        check_vma=False,
    )
```

```python
import functools

import jax
import jax.numpy as jnp
from jax import lax
from jax.experimental import pallas as pl
from jax.experimental.pallas import tpu as pltpu
from jax.sharding import PartitionSpec as P

ITERS = 2
MODE = 1024
RANK = 256
PLANE = 16
DEPTH = 8
SLAB = MODE // PLANE
BLK = 256
EARLY = 48
LATE = SLAB - EARLY
SLOTS = ((0, 0), (0, 1), (0, 2), (0, 3), (1, 3), (1, 1), (1, 2), (2, 2), (2, 3), (3, 3))
PACK = len(SLOTS) * 2 * BLK
HALF = PACK // 2
PLAN = ((0, 6 * BLK, 16), (6 * BLK, 4 * BLK, 8))
SEQUENCE = (0, 1, 0, 1, 0, 1, 0, 1, 0, 1, 1, 0, 1, 1)
ZORDER = (4, 3, 5, 2, 6, 1, 7)
MESH = pl.DeviceIdType.MESH
F32 = jnp.float32
BF16 = jnp.bfloat16
HI = lax.Precision.HIGHEST


def split(x):
    hi = x.astype(BF16)
    return hi, (x - hi.astype(F32)).astype(BF16)


def dot_nt(a, b):
    return lax.dot_general(a, b, (((1,), (1,)), ((), ())), preferred_element_type=F32)


def dot_nn(a, b, precision=None):
    return lax.dot_general(a, b, (((1,), (0,)), ((), ())), precision=precision, preferred_element_type=F32)


def dot_tn(a, b, precision=None):
    return lax.dot_general(a, b, (((0,), (0,)), ((), ())), precision=precision, preferred_element_type=F32)


def plane_peer(o):
    me = lax.axis_index("gx")
    x, y = me // 4, me % 4
    dx, dy = o // 4, o % 4
    to = ((x + dx) % 4) * 4 + (y + dy) % 4
    frm = ((x + 4 - dx) % 4) * 4 + (y + 4 - dy) % 4
    return to, frm


ORDER = (1, 3, 4, 12, 5, 7, 13, 15, 2, 8, 6, 14, 9, 11, 10)
RING = (1, 3, 2)


def gram_kernel(field, start, hs, ls, g_out, sh, sl, first, then, fib, p, a1, r0, ra, a2, rb, zin, rz, a3, zout,
                s_fib, v_fib, s_0, v_0, s_a, v_a, s_b, v_b, s_z, v_z, s_w, v_w,
                s_c, v_c, s_d, v_d, s_5, v_5, loc):
    me = lax.axis_index("gx")
    core = lax.axis_index("gy")
    z = lax.axis_index("gz")
    x, y = me // 4, me % 4
    barrier = pltpu.get_barrier_semaphore()
    for o in range(1, PLANE):
        pl.semaphore_signal(barrier, inc=1, device_id={"gx": plane_peer(o)[0]}, device_id_type=MESH)
    for o in range(1, DEPTH):
        pl.semaphore_signal(barrier, inc=1, device_id={"gz": (z + o) % DEPTH}, device_id_type=MESH)
    pl.semaphore_signal(barrier, inc=1, device_id={"gy": 1 - core}, device_id_type=MESH)
    pl.semaphore_wait(barrier, PLANE - 1 + DEPTH - 1 + 1)

    def send(src, dst, s_sem, v_sem, device):
        c = pltpu.make_async_remote_copy(
            src_ref=src, dst_ref=dst, send_sem=s_sem, recv_sem=v_sem, device_id=device, device_id_type=MESH)
        c.start()
        return c

    spans = ((0, EARLY), (EARLY, LATE))
    order = [a + core * (b - a) for a, b in zip(ORDER, ORDER[::-1])]

    def fibers(r, i):
        to, _ = plane_peer(order[i])
        at, n = spans[r]
        return send(field.at[to // 8, pl.ds(at, n), to % 8], fib.at[pl.ds(me * SLAB + at, n)],
                    s_fib.at[r], v_fib.at[r, i], {"gx": to})

    rounds = [[fibers(r, i) for i in range(PLANE - 1)] for r in range(2)]
    own = pltpu.make_async_copy(field.at[me // 8, :, me % 8], fib.at[pl.ds(me * SLAB, SLAB)], loc.at[0])
    own.start()
    begin = (pltpu.make_async_copy(start.at[:, pl.ds(0, EARLY)], first, loc.at[1]),
             pltpu.make_async_copy(start.at[:, pl.ds(EARLY, LATE)], then, loc.at[2]))
    for c in begin:
        c.start()
    zin[...] = jnp.zeros_like(zin)

    flat = fib.reshape(MODE * 8, 128)

    def halves(slab, r):
        at, n = spans[r]
        top = (slab * SLAB + at) * 8
        rows = pl.ds(pl.multiple_of(r * PLANE * EARLY + slab * n, LATE), n)
        for k in range(8):
            hi, lo = split(flat[pl.ds(top + k, n, stride=8), :])
            hs[rows, k * 128:(k + 1) * 128] = hi
            ls[rows, k * 128:(k + 1) * 128] = lo

    own.wait()
    halves(me, 0)
    halves(me, 1)
    for c in begin:
        c.wait()
    hi, lo = split(jnp.concatenate(
        [first[...].reshape(PLANE * EARLY, RANK), then[...].reshape(PLANE * LATE, RANK)], axis=0).T)
    sh[...] = hi
    sl[...] = lo

    def block(s):
        a, b = SLOTS[s]
        ha, la = hs[a * BLK:(a + 1) * BLK, :], ls[a * BLK:(a + 1) * BLK, :]
        hb, lb = hs[b * BLK:(b + 1) * BLK, :], ls[b * BLK:(b + 1) * BLK, :]
        acc = dot_nt(ha, hb) + (dot_nt(ha, lb) + dot_nt(la, hb))
        p[s * 512:s * 512 + 256, :] = acc[:, :128]
        p[s * 512 + 256:s * 512 + 512, :] = acc[:, 128:]

    mine = core * HALF
    other = {"gy": 1 - core}
    dims = ((x, y), (y, x))

    def ring(t, stage, o):
        if (t == 0) == (stage == 0):
            to = (x + o) % 4
            return {"gx": to * 4 + y}, to
        to = (y + o) % 4
        return {"gx": x * 4 + to}, to

    def drain(like, sem):
        pltpu.make_async_copy(like, like, sem).wait()

    def reduce_chunk(c):
        base, size, sub = PLAN[c]
        part, qa, qb = size // 2, size // 8, size // 32
        all_a, all_b = ra.at[c, :, :, pl.ds(0, qa)], rb.at[c, :, :, pl.ds(0, qb)]
        all_z = rz.at[c, pl.ds(0, DEPTH - 1), pl.ds(0, sub)]
        w = send(p.at[pl.ds((1 - core) * HALF + base, size)], r0.at[c, pl.ds(0, size)], s_0.at[c], v_0.at[c], other)
        yield
        w.wait_recv()
        a1[c, :size] = p[pl.ds(pl.multiple_of(mine + base, 512), size), :] + r0[c, :size]
        for o in RING:
            for t in range(2):
                dev, i = ring(t, 0, o)
                send(a1.at[c, pl.ds(t * part + i * qa, qa)], ra.at[c, t, o - 1, pl.ds(0, qa)],
                     s_a.at[c], v_a.at[c], dev)
        w.wait_send()
        yield
        drain(all_a, v_a.at[c])
        for t in range(2):
            a2[c, t, :qa] = (a1[c, pl.ds(pl.multiple_of(t * part + dims[t][0] * qa, 64), qa), :]
                             + ra[c, t, 0, :qa] + ra[c, t, 1, :qa] + ra[c, t, 2, :qa])
        for o in RING:
            for t in range(2):
                dev, j = ring(t, 1, o)
                send(a2.at[c, t, pl.ds(j * qb, qb)], rb.at[c, t, o - 1, pl.ds(0, qb)], s_b.at[c], v_b.at[c], dev)
        drain(all_a, s_a.at[c])
        yield
        drain(all_b, v_b.at[c])
        for t in range(2):
            zin[c, t * qb:(t + 1) * qb, :] = (a2[c, t, pl.ds(pl.multiple_of(dims[t][1] * qb, 16), qb), :]
                                              + rb[c, t, 0, :qb] + rb[c, t, 1, :qb] + rb[c, t, 2, :qb])
        for o in ZORDER:
            to = (z + o) % DEPTH
            send(zin.at[c, pl.ds(to * sub, sub)], rz.at[c, o - 1, pl.ds(0, sub)], s_z.at[c], v_z.at[c], {"gz": to})
        drain(all_b, s_b.at[c])
        yield
        drain(all_z, v_z.at[c])
        at = pl.ds(pl.multiple_of(z * sub, sub), sub)
        acc = zin[c, at, :]
        for o in range(1, DEPTH):
            acc = acc + rz[c, o - 1, :sub]
        a3[c, :sub] = acc
        for o in ZORDER:
            send(a3.at[c, pl.ds(0, sub)], zout.at[c, at], s_w.at[c], v_w.at[c], {"gz": (z + o) % DEPTH})
        zout[c, at, :] = acc
        drain(all_z, s_z.at[c])
        yield
        drain(all_z, v_w.at[c])
        for o in RING:
            for t in range(2):
                dev, _ = ring(t, 1, o)
                to = pl.ds(mine + base + t * part + dims[t][0] * qa + dims[t][1] * qb, qb)
                send(zout.at[c, pl.ds(t * qb, qb)], g_out.at[to], s_c.at[c], v_c.at[c], dev)
        for t in range(2):
            to = pl.multiple_of(mine + base + t * part + dims[t][0] * qa + dims[t][1] * qb, 16)
            g_out[pl.ds(to, qb), :] = zout[c, t * qb:(t + 1) * qb, :]
        drain(all_z, s_w.at[c])
        yield
        drain(all_b, v_c.at[c])
        for o in RING:
            for t in range(2):
                dev, _ = ring(t, 0, o)
                to = pl.ds(mine + base + t * part + dims[t][0] * qa, qa)
                send(g_out.at[to], g_out.at[to], s_d.at[c], v_d.at[c], dev)
        drain(all_b, s_c.at[c])
        yield
        drain(all_a, v_d.at[c])
        to = pl.ds(mine + base, size)
        w = send(g_out.at[to], g_out.at[to], s_5.at[c], v_5.at[c], other)
        drain(all_a, s_d.at[c])
        yield
        w.wait_recv()
        w.wait_send()
        yield

    one, two = reduce_chunk(0), reduce_chunk(1)
    for i, c in enumerate(rounds[0]):
        c.wait_recv()
        halves(plane_peer(order[i])[1], 0)
    for s in (0, 1, 2, 5, 6, 7):
        block(s)
    next(one)
    for i, c in enumerate(rounds[1]):
        c.wait_recv()
        halves(plane_peer(order[i])[1], 1)
        if i == 4:
            next(one)
    for s in (3, 4):
        block(s)
    next(one)
    for s in (8, 9):
        block(s)
    next(two)
    for r, (_, n) in enumerate(spans):
        drain(fib.at[pl.ds(0, (PLANE - 1) * n)], s_fib.at[r])
    for who in SEQUENCE:
        next((one, two)[who])


def gram_call(field, start):
    dma = pltpu.SemaphoreType.DMA
    vm = pltpu.VMEM
    whole = pl.BlockSpec(memory_space=pltpu.VMEM)
    return pl.pallas_call(
        gram_kernel,
        out_shape=(
            jax.ShapeDtypeStruct((MODE, 1024), BF16),
            jax.ShapeDtypeStruct((MODE, 1024), BF16),
            jax.ShapeDtypeStruct((PACK, 128), F32),
            jax.ShapeDtypeStruct((RANK, MODE), BF16),
            jax.ShapeDtypeStruct((RANK, MODE), BF16),
        ),
        in_specs=[pl.BlockSpec(memory_space=pltpu.HBM)] * 2,
        out_specs=(whole,) * 5,
        scratch_shapes=[
            vm((PLANE, EARLY, RANK), F32), vm((PLANE, LATE, RANK), F32), vm((MODE, 8, 128), F32), vm((PACK, 128), F32),
            vm((2, 1536, 128), F32), vm((2, 1536, 128), F32),
            vm((2, 2, 3, 192, 128), F32), vm((2, 2, 192, 128), F32), vm((2, 2, 3, 48, 128), F32),
            vm((2, 128, 128), F32), vm((2, DEPTH - 1, 16, 128), F32), vm((2, 16, 128), F32), vm((2, 128, 128), F32),
            dma((2,)), dma((2, PLANE)), *[dma((2,))] * 16, dma((3,)),
        ],
        compiler_params=pltpu.CompilerParams(
            collective_id=0, has_side_effects=True, vmem_limit_bytes=40 << 20),
        name="gram",
    )(field, start)


NB = 64


def recip(x):
    return 1.0 / x


def row_of(x, k):
    return jnp.broadcast_to(x[k:k + 1, :], (8, 128))


def lower_inverse(w):
    lane = lax.broadcasted_iota(jnp.int32, (8, 128), 1)
    row = lax.broadcasted_iota(jnp.int32, (8, 128), 0)
    nv = NB // 8
    chunks = RANK // 128
    for top in range(0, RANK, NB):
        pc = top // 128
        off = top % 128
        d = [[w[top + 8 * u:top + 8 * u + 8, c * 128:(c + 1) * 128] for c in range(chunks)] for u in range(nv)]
        scale = []
        for v in range(nv):
            j0 = off + 8 * v
            e = [jnp.broadcast_to(d[v][pc][:, j0 + k:j0 + k + 1], (8, 128)) for k in range(8)]
            group = (lane >= j0) & (lane < j0 + 8)
            inv, b = [], {}
            dv = jnp.ones((8, 128), F32)
            for k in range(8):
                piv = row_of(e[k], k)
                dv = jnp.where(row == k, piv, dv)
                inv.append(recip(piv))
                f = jnp.where(row > k, e[k] * inv[k], 0.0)
                for k2 in range(k + 1, 8):
                    b[k, k2] = row_of(e[k2], k)
                    e[k2] = e[k2] - f * b[k, k2]
                for c in range(chunks):
                    prow = row_of(d[v][c], k)
                    if c == pc:
                        prow = jnp.where(lane == j0 + k, 1.0, prow)
                        base = jnp.where((lane == j0 + k) & (row > k), 0.0, d[v][c])
                    else:
                        base = d[v][c]
                    d[v][c] = base - f * prow
            scale.append(lax.rsqrt(dv))
            unit = jnp.where(lane == j0 + row, 1.0, jnp.where(lane < j0 + row, d[v][pc], 0.0))
            d[v][pc] = jnp.where(group, unit, d[v][pc])
            for u in range(v + 1, nv):
                e = [jnp.broadcast_to(d[u][pc][:, j0 + k:j0 + k + 1], (8, 128)) for k in range(8)]
                f = []
                for k in range(8):
                    f.append(e[k] * inv[k])
                    for k2 in range(k + 1, 8):
                        e[k2] = e[k2] - f[k] * b[k, k2]
                for c in range(chunks):
                    t = f[0] * row_of(d[v][c], 0)
                    for k in range(1, 8):
                        t = t + f[k] * row_of(d[v][c], k)
                    d[u][c] = (jnp.where(group, 0.0, d[u][c]) if c == pc else d[u][c]) - t
        cols = []
        for c in range(chunks):
            rows = []
            for u in range(nv):
                x = d[u][c]
                if c == pc:
                    x = jnp.where((lane > off + 8 * u + row) & (lane < off + NB), 0.0, x)
                rows.append(x * scale[u])
            cols.append(jnp.concatenate(rows, axis=0))
        done = jnp.concatenate(cols, axis=1)
        w[top:top + NB, :] = done
        if top + NB < RANK:
            hi, lo = split(done)
            left = jnp.concatenate([hi, hi, lo], axis=0)[:, top + NB:]
            t = dot_tn(left, jnp.concatenate([hi, lo, hi], axis=0))
            for c in range(chunks):
                base = w[top + NB:, c * 128:(c + 1) * 128]
                if c == pc:
                    at = lax.broadcasted_iota(jnp.int32, base.shape, 1)
                    base = jnp.where((at >= off) & (at < off + NB), 0.0, base)
                w[top + NB:, c * 128:(c + 1) * 128] = base - t[:, c * 128:(c + 1) * 128]


def basis_kernel(g_ref, sh_ref, sl_ref, f_out, bh_out, bl_out, gh, gl, w, wide, turn):
    for s, (a, b) in enumerate(SLOTS):
        for e in range(2):
            hi, lo = split(g_ref[s * 512 + e * 256:s * 512 + e * 256 + 256, :])
            cols = slice(b * BLK + e * 128, b * BLK + e * 128 + 128)
            gh[a * BLK:(a + 1) * BLK, cols] = hi
            gl[a * BLK:(a + 1) * BLK, cols] = lo
    lanes = lax.broadcasted_iota(jnp.int32, (RANK, RANK), 1)
    rows = lax.broadcasted_iota(jnp.int32, (RANK, RANK), 0)
    bh, bl = sh_ref[...], sl_ref[...]
    for step in range(ITERS):
        image = []
        for b in range(4):
            n = (b + 1) * BLK
            cols = slice(b * BLK, n)
            acc = (dot_nn(bh[:, :n], gh[:n, cols])
                   + (dot_nn(bh[:, :n], gl[:n, cols]) + dot_nn(bl[:, :n], gh[:n, cols])))
            if n < MODE:
                acc = acc + (dot_nt(bh[:, n:], gh[cols, n:])
                             + (dot_nt(bh[:, n:], gl[cols, n:]) + dot_nt(bl[:, n:], gh[cols, n:])))
            image.append(acc)
        ih, il = split(jnp.concatenate(image, axis=1))
        w[...] = dot_nt(ih, ih) + (dot_nt(ih, il) + dot_nt(il, ih))
        lower_inverse(w)
        vh, vl = split(jnp.where(lanes <= rows, w[...], 0.0))
        basis = dot_nn(vh, ih) + (dot_nn(vh, il) + dot_nn(vl, ih))
        bh, bl = split(basis)
    bh_out[...] = bh
    bl_out[...] = bl
    me = lax.axis_index("gx")
    wide[...] = basis
    at = me * EARLY // 128
    turn[:RANK, :] = wide[:, pl.ds(pl.multiple_of(at * 128, 128), 256)].T
    f_out[:EARLY, :] = turn[pl.ds(pl.multiple_of(me * EARLY - at * 128, 16), EARLY), :]
    at = (PLANE * EARLY + me * LATE) // 128
    turn[RANK:, :] = wide[:, pl.ds(pl.multiple_of(at * 128, 128), 128)].T
    f_out[EARLY:, :] = turn[pl.ds(pl.multiple_of(RANK + PLANE * EARLY + me * LATE - at * 128, 16), LATE), :]


def basis_call(packed, start_h, start_l):
    return pl.pallas_call(
        basis_kernel,
        out_shape=(
            jax.ShapeDtypeStruct((SLAB, RANK), F32),
            jax.ShapeDtypeStruct((RANK, MODE), BF16),
            jax.ShapeDtypeStruct((RANK, MODE), BF16),
        ),
        scratch_shapes=[pltpu.VMEM((MODE, MODE), BF16), pltpu.VMEM((MODE, MODE), BF16),
                        pltpu.VMEM((RANK, RANK), F32), pltpu.VMEM((RANK, MODE), F32),
                        pltpu.VMEM((384, RANK), F32)],
        compiler_params=pltpu.CompilerParams(vmem_limit_bytes=40 << 20),
        name="basis",
    )(packed, start_h, start_l)


def core_kernel(bh, bl, h, l, out, res, s_sem, v_sem, loc):
    me = lax.axis_index("gx")
    barrier = pltpu.get_barrier_semaphore()
    for o in range(1, PLANE):
        pl.semaphore_signal(barrier, inc=1, device_id={"gx": plane_peer(o)[0]}, device_id_type=MESH)
    x = me // 4
    rank = RANK // PLANE
    wide = 4 * rank
    flat = res.reshape(RANK * 8, 128)
    for first, steps in enumerate(((1, 3), (2, 0))):
        places = [pl.multiple_of(((x + dx) % 4) * wide, wide) for dx in steps]
        rows_h = jnp.concatenate([bh[pl.ds(r, wide), :] for r in places], axis=0)
        rows_l = jnp.concatenate([bl[pl.ds(r, wide), :] for r in places], axis=0)
        for yy in range(4):
            cols = slice(yy * 256, yy * 256 + 256)
            acc = dot_nn(rows_h, h[:, cols]) + (dot_nn(rows_h, l[:, cols]) + dot_nn(rows_l, h[:, cols]))
            for n, r in enumerate(places):
                for e in range(2):
                    flat[pl.ds(r * 8 + 2 * yy + e, wide, stride=8), :] = (
                        acc[n * wide:(n + 1) * wide, e * 128:(e + 1) * 128])
        if first == 0:
            pl.semaphore_wait(barrier, PLANE - 1)
        for dy in (1, 3, 2, 0):
            for dx in steps:
                o = dx * 4 + dy
                if o == 0:
                    continue
                to, _ = plane_peer(o)
                c = pltpu.make_async_remote_copy(
                    src_ref=res.at[pl.ds(to * rank, rank)], dst_ref=out.at[me // 8, :, me % 8],
                    send_sem=s_sem, recv_sem=v_sem, device_id={"gx": to}, device_id_type=MESH)
                c.start()
    own = pltpu.make_async_copy(res.at[pl.ds(me * rank, rank)], out.at[me // 8, :, me % 8], loc)
    own.start()
    like = res.at[pl.ds(0, (PLANE - 1) * rank)]
    pltpu.make_async_copy(like, like, v_sem).wait()
    pltpu.make_async_copy(like, like, s_sem).wait()
    own.wait()


def core_call(bh, bl, h, l, comps):
    vmem = pl.BlockSpec(memory_space=pltpu.VMEM)
    return pl.pallas_call(
        core_kernel,
        out_shape=jax.ShapeDtypeStruct((comps, RANK // PLANE, 8, 8, 128), F32),
        in_specs=[vmem] * 4,
        out_specs=pl.BlockSpec(memory_space=pl.ANY),
        scratch_shapes=[pltpu.VMEM((RANK, 8, 128), F32), pltpu.SemaphoreType.DMA, pltpu.SemaphoreType.DMA,
                        pltpu.SemaphoreType.DMA],
        compiler_params=pltpu.CompilerParams(
            collective_id=1, has_side_effects=True, vmem_limit_bytes=32 << 20),
        name="core",
    )(bh, bl, h, l)


def per_device(field, start_basis):
    comps, slab, cells_y, cells_z = field.shape
    h, l, packed, start_h, start_l = gram_call(
        pltpu.with_memory_space_constraint(field.reshape(comps, slab, cells_y // 8, 8, cells_z), pltpu.HBM),
        pltpu.with_memory_space_constraint(start_basis.reshape(PLANE, SLAB, RANK), pltpu.HBM))
    factor, bh, bl = basis_call(packed, start_h, start_l)
    core = core_call(bh, bl, h, l, comps)
    return (factor, core.reshape(comps, RANK // PLANE, cells_y, cells_z))


def solution(mesh):
    placed = (P(None, "gx", "gy", "gz"), P())
    return jax.shard_map(
        per_device,
        mesh=mesh,
        in_specs=placed,
        out_specs=(P("gx", None), P(None, "gx", "gy", "gz")),
        check_vma=False,
    )
```

```python
import functools

import jax
import jax.numpy as jnp
from jax import lax
from jax.experimental import pallas as pl
from jax.experimental.pallas import tpu as pltpu
from jax.sharding import PartitionSpec as P

ITERS = 2
MODE = 1024
RANK = 256
PLANE = 16
DEPTH = 8
SLAB = MODE // PLANE
BLK = 256
EARLY = 48
LATE = SLAB - EARLY
SLOTS = ((0, 0), (0, 1), (0, 2), (0, 3), (1, 3), (1, 1), (1, 2), (2, 2), (2, 3), (3, 3))
PACK = len(SLOTS) * 2 * BLK
HALF = PACK // 2
PLAN = ((0, 6 * BLK, 16), (6 * BLK, 4 * BLK, 8))
SEQUENCE = (1, 0, 1, 0, 1, 0, 1, 0, 1, 0, 1, 0, 1, 0, 1)
ZORDER = (4, 3, 5, 2, 6, 1, 7)
MESH = pl.DeviceIdType.MESH
F32 = jnp.float32
BF16 = jnp.bfloat16
HI = lax.Precision.HIGHEST


def split(x):
    hi = x.astype(BF16)
    return hi, (x - hi.astype(F32)).astype(BF16)


def dot_nt(a, b):
    return lax.dot_general(a, b, (((1,), (1,)), ((), ())), preferred_element_type=F32)


def dot_nn(a, b, precision=None):
    return lax.dot_general(a, b, (((1,), (0,)), ((), ())), precision=precision, preferred_element_type=F32)


def dot_tn(a, b, precision=None):
    return lax.dot_general(a, b, (((0,), (0,)), ((), ())), precision=precision, preferred_element_type=F32)


def plane_peer(o):
    me = lax.axis_index("gx")
    x, y = me // 4, me % 4
    dx, dy = o // 4, o % 4
    to = ((x + dx) % 4) * 4 + (y + dy) % 4
    frm = ((x + 4 - dx) % 4) * 4 + (y + 4 - dy) % 4
    return to, frm


ORDER = (1, 3, 4, 12, 5, 7, 13, 15, 2, 8, 6, 14, 9, 11, 10)
RING = (1, 3, 2)


def gram_kernel(field, start, hs, ls, g_out, sh, sl, first, then, fib, p, a1, r0, ra, a2, rb, zin, rz, a3, zout,
                s_fib, v_fib, s_0, v_0, s_a, v_a, s_b, v_b, s_z, v_z, s_w, v_w,
                s_c, v_c, s_d, v_d, s_5, v_5, loc):
    me = lax.axis_index("gx")
    core = lax.axis_index("gy")
    z = lax.axis_index("gz")
    x, y = me // 4, me % 4
    barrier = pltpu.get_barrier_semaphore()
    for o in range(1, PLANE):
        pl.semaphore_signal(barrier, inc=1, device_id={"gx": plane_peer(o)[0]}, device_id_type=MESH)
    for o in range(1, DEPTH):
        pl.semaphore_signal(barrier, inc=1, device_id={"gz": (z + o) % DEPTH}, device_id_type=MESH)
    pl.semaphore_signal(barrier, inc=1, device_id={"gy": 1 - core}, device_id_type=MESH)
    pl.semaphore_wait(barrier, PLANE - 1 + DEPTH - 1 + 1)

    def send(src, dst, s_sem, v_sem, device):
        c = pltpu.make_async_remote_copy(
            src_ref=src, dst_ref=dst, send_sem=s_sem, recv_sem=v_sem, device_id=device, device_id_type=MESH)
        c.start()
        return c

    spans = ((0, EARLY), (EARLY, LATE))
    order = [a + core * (b - a) for a, b in zip(ORDER, ORDER[::-1])]

    def fibers(r, i):
        to, _ = plane_peer(order[i])
        at, n = spans[r]
        return send(field.at[to // 8, pl.ds(at, n), to % 8], fib.at[pl.ds(me * SLAB + at, n)],
                    s_fib.at[r], v_fib.at[r, i], {"gx": to})

    rounds = [[fibers(r, i) for i in range(PLANE - 1)] for r in range(2)]
    own = pltpu.make_async_copy(field.at[me // 8, :, me % 8], fib.at[pl.ds(me * SLAB, SLAB)], loc.at[0])
    own.start()
    begin = (pltpu.make_async_copy(start.at[:, pl.ds(0, EARLY)], first, loc.at[1]),
             pltpu.make_async_copy(start.at[:, pl.ds(EARLY, LATE)], then, loc.at[2]))
    for c in begin:
        c.start()
    zin[...] = jnp.zeros_like(zin)

    flat = fib.reshape(MODE * 8, 128)

    def halves(slab, r):
        at, n = spans[r]
        top = (slab * SLAB + at) * 8
        rows = pl.ds(pl.multiple_of(r * PLANE * EARLY + slab * n, LATE), n)
        for k in range(8):
            hi, lo = split(flat[pl.ds(top + k, n, stride=8), :])
            hs[rows, k * 128:(k + 1) * 128] = hi
            ls[rows, k * 128:(k + 1) * 128] = lo

    own.wait()
    halves(me, 0)
    halves(me, 1)
    for c in begin:
        c.wait()
    hi, lo = split(jnp.concatenate(
        [first[...].reshape(PLANE * EARLY, RANK), then[...].reshape(PLANE * LATE, RANK)], axis=0).T)
    sh[...] = hi
    sl[...] = lo

    def block(s):
        a, b = SLOTS[s]
        ha, la = hs[a * BLK:(a + 1) * BLK, :], ls[a * BLK:(a + 1) * BLK, :]
        hb, lb = hs[b * BLK:(b + 1) * BLK, :], ls[b * BLK:(b + 1) * BLK, :]
        acc = dot_nt(ha, hb) + (dot_nt(ha, lb) + dot_nt(la, hb))
        p[s * 512:s * 512 + 256, :] = acc[:, :128]
        p[s * 512 + 256:s * 512 + 512, :] = acc[:, 128:]

    mine = core * HALF
    other = {"gy": 1 - core}
    dims = ((x, y), (y, x))

    def ring(t, stage, o):
        if (t == 0) == (stage == 0):
            to = (x + o) % 4
            return {"gx": to * 4 + y}, to
        to = (y + o) % 4
        return {"gx": x * 4 + to}, to

    def drain(like, sem):
        pltpu.make_async_copy(like, like, sem).wait()

    def reduce_chunk(c):
        base, size, sub = PLAN[c]
        part, qa, qb = size // 2, size // 8, size // 32
        all_a, all_b = ra.at[c, :, :, pl.ds(0, qa)], rb.at[c, :, :, pl.ds(0, qb)]
        all_z = rz.at[c, pl.ds(0, DEPTH - 1), pl.ds(0, sub)]
        w = send(p.at[pl.ds((1 - core) * HALF + base, size)], r0.at[c, pl.ds(0, size)], s_0.at[c], v_0.at[c], other)
        yield
        w.wait_recv()
        a1[c, :size] = p[pl.ds(pl.multiple_of(mine + base, 512), size), :] + r0[c, :size]
        for o in RING:
            for t in range(2):
                dev, i = ring(t, 0, o)
                send(a1.at[c, pl.ds(t * part + i * qa, qa)], ra.at[c, t, o - 1, pl.ds(0, qa)],
                     s_a.at[c], v_a.at[c], dev)
        w.wait_send()
        yield
        drain(all_a, v_a.at[c])
        for t in range(2):
            a2[c, t, :qa] = (a1[c, pl.ds(pl.multiple_of(t * part + dims[t][0] * qa, 64), qa), :]
                             + ra[c, t, 0, :qa] + ra[c, t, 1, :qa] + ra[c, t, 2, :qa])
        for o in RING:
            for t in range(2):
                dev, j = ring(t, 1, o)
                send(a2.at[c, t, pl.ds(j * qb, qb)], rb.at[c, t, o - 1, pl.ds(0, qb)], s_b.at[c], v_b.at[c], dev)
        drain(all_a, s_a.at[c])
        yield
        drain(all_b, v_b.at[c])
        for t in range(2):
            zin[c, t * qb:(t + 1) * qb, :] = (a2[c, t, pl.ds(pl.multiple_of(dims[t][1] * qb, 16), qb), :]
                                              + rb[c, t, 0, :qb] + rb[c, t, 1, :qb] + rb[c, t, 2, :qb])
        for o in ZORDER:
            to = (z + o) % DEPTH
            send(zin.at[c, pl.ds(to * sub, sub)], rz.at[c, o - 1, pl.ds(0, sub)], s_z.at[c], v_z.at[c], {"gz": to})
        drain(all_b, s_b.at[c])
        yield
        drain(all_z, v_z.at[c])
        at = pl.ds(pl.multiple_of(z * sub, sub), sub)
        acc = zin[c, at, :]
        for o in range(1, DEPTH):
            acc = acc + rz[c, o - 1, :sub]
        a3[c, :sub] = acc
        for o in ZORDER:
            send(a3.at[c, pl.ds(0, sub)], zout.at[c, at], s_w.at[c], v_w.at[c], {"gz": (z + o) % DEPTH})
        zout[c, at, :] = acc
        drain(all_z, s_z.at[c])
        yield
        drain(all_z, v_w.at[c])
        for o in RING:
            for t in range(2):
                dev, _ = ring(t, 1, o)
                to = pl.ds(mine + base + t * part + dims[t][0] * qa + dims[t][1] * qb, qb)
                send(zout.at[c, pl.ds(t * qb, qb)], g_out.at[to], s_c.at[c], v_c.at[c], dev)
        for t in range(2):
            to = pl.multiple_of(mine + base + t * part + dims[t][0] * qa + dims[t][1] * qb, 16)
            g_out[pl.ds(to, qb), :] = zout[c, t * qb:(t + 1) * qb, :]
        drain(all_z, s_w.at[c])
        yield
        drain(all_b, v_c.at[c])
        for o in RING:
            for t in range(2):
                dev, _ = ring(t, 0, o)
                to = pl.ds(mine + base + t * part + dims[t][0] * qa, qa)
                send(g_out.at[to], g_out.at[to], s_d.at[c], v_d.at[c], dev)
        drain(all_b, s_c.at[c])
        yield
        drain(all_a, v_d.at[c])
        to = pl.ds(mine + base, size)
        w = send(g_out.at[to], g_out.at[to], s_5.at[c], v_5.at[c], other)
        drain(all_a, s_d.at[c])
        yield
        w.wait_recv()
        w.wait_send()
        yield

    one, two = reduce_chunk(0), reduce_chunk(1)
    for i, c in enumerate(rounds[0]):
        c.wait_recv()
        halves(plane_peer(order[i])[1], 0)
    for s in (0, 1, 2, 5, 6, 7):
        block(s)
    next(one)
    for i, c in enumerate(rounds[1]):
        c.wait_recv()
        halves(plane_peer(order[i])[1], 1)
        if i == 4:
            next(one)
    for s in (3, 4, 8, 9):
        block(s)
    next(two)
    for r, (_, n) in enumerate(spans):
        drain(fib.at[pl.ds(0, (PLANE - 1) * n)], s_fib.at[r])
    for who in SEQUENCE:
        next((one, two)[who])


def gram_call(field, start):
    dma = pltpu.SemaphoreType.DMA
    vm = pltpu.VMEM
    whole = pl.BlockSpec(memory_space=pltpu.VMEM)
    return pl.pallas_call(
        gram_kernel,
        out_shape=(
            jax.ShapeDtypeStruct((MODE, 1024), BF16),
            jax.ShapeDtypeStruct((MODE, 1024), BF16),
            jax.ShapeDtypeStruct((PACK, 128), F32),
            jax.ShapeDtypeStruct((RANK, MODE), BF16),
            jax.ShapeDtypeStruct((RANK, MODE), BF16),
        ),
        in_specs=[pl.BlockSpec(memory_space=pltpu.HBM)] * 2,
        out_specs=(whole,) * 5,
        scratch_shapes=[
            vm((PLANE, EARLY, RANK), F32), vm((PLANE, LATE, RANK), F32), vm((MODE, 8, 128), F32), vm((PACK, 128), F32),
            vm((2, 1536, 128), F32), vm((2, 1536, 128), F32),
            vm((2, 2, 3, 192, 128), F32), vm((2, 2, 192, 128), F32), vm((2, 2, 3, 48, 128), F32),
            vm((2, 128, 128), F32), vm((2, DEPTH - 1, 16, 128), F32), vm((2, 16, 128), F32), vm((2, 128, 128), F32),
            dma((2,)), dma((2, PLANE)), *[dma((2,))] * 16, dma((3,)),
        ],
        compiler_params=pltpu.CompilerParams(
            collective_id=0, has_side_effects=True, vmem_limit_bytes=40 << 20),
        name="gram",
    )(field, start)


NB = 64


def recip(x):
    return 1.0 / x


def row_of(x, k):
    return jnp.broadcast_to(x[k:k + 1, :], (8, 128))


def lower_inverse(w):
    lane = lax.broadcasted_iota(jnp.int32, (8, 128), 1)
    row = lax.broadcasted_iota(jnp.int32, (8, 128), 0)
    nv = NB // 8
    chunks = RANK // 128
    for top in range(0, RANK, NB):
        pc = top // 128
        off = top % 128
        d = [[w[top + 8 * u:top + 8 * u + 8, c * 128:(c + 1) * 128] for c in range(chunks)] for u in range(nv)]
        scale = []
        for v in range(nv):
            j0 = off + 8 * v
            e = [jnp.broadcast_to(d[v][pc][:, j0 + k:j0 + k + 1], (8, 128)) for k in range(8)]
            group = (lane >= j0) & (lane < j0 + 8)
            inv, b = [], {}
            dv = jnp.ones((8, 128), F32)
            for k in range(8):
                piv = row_of(e[k], k)
                dv = jnp.where(row == k, piv, dv)
                inv.append(recip(piv))
                f = jnp.where(row > k, e[k] * inv[k], 0.0)
                for k2 in range(k + 1, 8):
                    b[k, k2] = row_of(e[k2], k)
                    e[k2] = e[k2] - f * b[k, k2]
                for c in range(chunks):
                    prow = row_of(d[v][c], k)
                    if c == pc:
                        prow = jnp.where(lane == j0 + k, 1.0, prow)
                        base = jnp.where((lane == j0 + k) & (row > k), 0.0, d[v][c])
                    else:
                        base = d[v][c]
                    d[v][c] = base - f * prow
            scale.append(lax.rsqrt(dv))
            unit = jnp.where(lane == j0 + row, 1.0, jnp.where(lane < j0 + row, d[v][pc], 0.0))
            d[v][pc] = jnp.where(group, unit, d[v][pc])
            for u in range(v + 1, nv):
                e = [jnp.broadcast_to(d[u][pc][:, j0 + k:j0 + k + 1], (8, 128)) for k in range(8)]
                f = []
                for k in range(8):
                    f.append(e[k] * inv[k])
                    for k2 in range(k + 1, 8):
                        e[k2] = e[k2] - f[k] * b[k, k2]
                for c in range(chunks):
                    t = f[0] * row_of(d[v][c], 0)
                    for k in range(1, 8):
                        t = t + f[k] * row_of(d[v][c], k)
                    d[u][c] = (jnp.where(group, 0.0, d[u][c]) if c == pc else d[u][c]) - t
        cols = []
        for c in range(chunks):
            rows = []
            for u in range(nv):
                x = d[u][c]
                if c == pc:
                    x = jnp.where((lane > off + 8 * u + row) & (lane < off + NB), 0.0, x)
                rows.append(x * scale[u])
            cols.append(jnp.concatenate(rows, axis=0))
        done = jnp.concatenate(cols, axis=1)
        w[top:top + NB, :] = done
        if top + NB < RANK:
            hi, lo = split(done)
            left = jnp.concatenate([hi, hi, lo], axis=0)[:, top + NB:]
            t = dot_tn(left, jnp.concatenate([hi, lo, hi], axis=0))
            for c in range(chunks):
                base = w[top + NB:, c * 128:(c + 1) * 128]
                if c == pc:
                    at = lax.broadcasted_iota(jnp.int32, base.shape, 1)
                    base = jnp.where((at >= off) & (at < off + NB), 0.0, base)
                w[top + NB:, c * 128:(c + 1) * 128] = base - t[:, c * 128:(c + 1) * 128]


def basis_kernel(g_ref, sh_ref, sl_ref, f_out, bh_out, bl_out, gh, gl, w, wide, turn):
    for s, (a, b) in enumerate(SLOTS):
        for e in range(2):
            hi, lo = split(g_ref[s * 512 + e * 256:s * 512 + e * 256 + 256, :])
            cols = slice(b * BLK + e * 128, b * BLK + e * 128 + 128)
            gh[a * BLK:(a + 1) * BLK, cols] = hi
            gl[a * BLK:(a + 1) * BLK, cols] = lo
    lanes = lax.broadcasted_iota(jnp.int32, (RANK, RANK), 1)
    rows = lax.broadcasted_iota(jnp.int32, (RANK, RANK), 0)
    bh, bl = sh_ref[...], sl_ref[...]
    for step in range(ITERS):
        image = []
        for b in range(4):
            n = (b + 1) * BLK
            cols = slice(b * BLK, n)
            acc = (dot_nn(bh[:, :n], gh[:n, cols])
                   + (dot_nn(bh[:, :n], gl[:n, cols]) + dot_nn(bl[:, :n], gh[:n, cols])))
            if n < MODE:
                acc = acc + (dot_nt(bh[:, n:], gh[cols, n:])
                             + (dot_nt(bh[:, n:], gl[cols, n:]) + dot_nt(bl[:, n:], gh[cols, n:])))
            image.append(acc)
        ih, il = split(jnp.concatenate(image, axis=1))
        w[...] = dot_nt(ih, ih) + (dot_nt(ih, il) + dot_nt(il, ih))
        lower_inverse(w)
        vh, vl = split(jnp.where(lanes <= rows, w[...], 0.0))
        basis = dot_nn(vh, ih) + (dot_nn(vh, il) + dot_nn(vl, ih))
        bh, bl = split(basis)
    bh_out[...] = bh
    bl_out[...] = bl
    me = lax.axis_index("gx")
    wide[...] = basis
    at = me * EARLY // 128
    turn[:RANK, :] = wide[:, pl.ds(pl.multiple_of(at * 128, 128), 256)].T
    f_out[:EARLY, :] = turn[pl.ds(pl.multiple_of(me * EARLY - at * 128, 16), EARLY), :]
    at = (PLANE * EARLY + me * LATE) // 128
    turn[RANK:, :] = wide[:, pl.ds(pl.multiple_of(at * 128, 128), 128)].T
    f_out[EARLY:, :] = turn[pl.ds(pl.multiple_of(RANK + PLANE * EARLY + me * LATE - at * 128, 16), LATE), :]


def basis_call(packed, start_h, start_l):
    return pl.pallas_call(
        basis_kernel,
        out_shape=(
            jax.ShapeDtypeStruct((SLAB, RANK), F32),
            jax.ShapeDtypeStruct((RANK, MODE), BF16),
            jax.ShapeDtypeStruct((RANK, MODE), BF16),
        ),
        scratch_shapes=[pltpu.VMEM((MODE, MODE), BF16), pltpu.VMEM((MODE, MODE), BF16),
                        pltpu.VMEM((RANK, RANK), F32), pltpu.VMEM((RANK, MODE), F32),
                        pltpu.VMEM((384, RANK), F32)],
        compiler_params=pltpu.CompilerParams(vmem_limit_bytes=40 << 20),
        name="basis",
    )(packed, start_h, start_l)


def core_kernel(bh, bl, h, l, out, res, s_sem, v_sem, loc):
    me = lax.axis_index("gx")
    barrier = pltpu.get_barrier_semaphore()
    for o in range(1, PLANE):
        pl.semaphore_signal(barrier, inc=1, device_id={"gx": plane_peer(o)[0]}, device_id_type=MESH)
    x = me // 4
    rank = RANK // PLANE
    wide = 4 * rank
    flat = res.reshape(RANK * 8, 128)
    for first, steps in enumerate(((1, 3), (2, 0))):
        places = [pl.multiple_of(((x + dx) % 4) * wide, wide) for dx in steps]
        rows_h = jnp.concatenate([bh[pl.ds(r, wide), :] for r in places], axis=0)
        rows_l = jnp.concatenate([bl[pl.ds(r, wide), :] for r in places], axis=0)
        for yy in range(4):
            cols = slice(yy * 256, yy * 256 + 256)
            acc = dot_nn(rows_h, h[:, cols]) + (dot_nn(rows_h, l[:, cols]) + dot_nn(rows_l, h[:, cols]))
            for n, r in enumerate(places):
                for e in range(2):
                    flat[pl.ds(r * 8 + 2 * yy + e, wide, stride=8), :] = (
                        acc[n * wide:(n + 1) * wide, e * 128:(e + 1) * 128])
        if first == 0:
            pl.semaphore_wait(barrier, PLANE - 1)
        for dy in (1, 3, 2, 0):
            for dx in steps:
                o = dx * 4 + dy
                if o == 0:
                    continue
                to, _ = plane_peer(o)
                c = pltpu.make_async_remote_copy(
                    src_ref=res.at[pl.ds(to * rank, rank)], dst_ref=out.at[me // 8, :, me % 8],
                    send_sem=s_sem, recv_sem=v_sem, device_id={"gx": to}, device_id_type=MESH)
                c.start()
    own = pltpu.make_async_copy(res.at[pl.ds(me * rank, rank)], out.at[me // 8, :, me % 8], loc)
    own.start()
    like = res.at[pl.ds(0, (PLANE - 1) * rank)]
    pltpu.make_async_copy(like, like, v_sem).wait()
    pltpu.make_async_copy(like, like, s_sem).wait()
    own.wait()


def core_call(bh, bl, h, l, comps):
    vmem = pl.BlockSpec(memory_space=pltpu.VMEM)
    return pl.pallas_call(
        core_kernel,
        out_shape=jax.ShapeDtypeStruct((comps, RANK // PLANE, 8, 8, 128), F32),
        in_specs=[vmem] * 4,
        out_specs=pl.BlockSpec(memory_space=pl.ANY),
        scratch_shapes=[pltpu.VMEM((RANK, 8, 128), F32), pltpu.SemaphoreType.DMA, pltpu.SemaphoreType.DMA,
                        pltpu.SemaphoreType.DMA],
        compiler_params=pltpu.CompilerParams(
            collective_id=1, has_side_effects=True, vmem_limit_bytes=32 << 20),
        name="core",
    )(bh, bl, h, l)


def per_device(field, start_basis):
    comps, slab, cells_y, cells_z = field.shape
    h, l, packed, start_h, start_l = gram_call(
        pltpu.with_memory_space_constraint(field.reshape(comps, slab, cells_y // 8, 8, cells_z), pltpu.HBM),
        pltpu.with_memory_space_constraint(start_basis.reshape(PLANE, SLAB, RANK), pltpu.HBM))
    factor, bh, bl = basis_call(packed, start_h, start_l)
    core = core_call(bh, bl, h, l, comps)
    return (factor, core.reshape(comps, RANK // PLANE, cells_y, cells_z))


def solution(mesh):
    placed = (P(None, "gx", "gy", "gz"), P())
    return jax.shard_map(
        per_device,
        mesh=mesh,
        in_specs=placed,
        out_specs=(P("gx", None), P(None, "gx", "gy", "gz")),
        check_vma=False,
    )
```
